32 devices in a mesh: parts: 2 (over x), img: 16 (over z, y, core).
Axes of the slice: x: 2, y: 2, z: 4, core: 2. Of those that a mesh axis runs over, the one named last changes fastest.
Arguments:
- images: bfloat16 [2048, 16384], P(('parts', 'img')), parts along dimension 0, may hold values from -28 to 28
- groups: int32 [2048], P(('parts', 'img')), parts along dimension 0, may hold values from 0 to 7
- shifts: int32 [18, 2], P('parts'), parts along dimension 0, may hold values from -3 to 3
- volume: bfloat16 [32768, 256], P(('parts', 'img')), parts along dimension 0, may hold values from -6 to 6
- owner: int32 [8192, 1], P('parts'), parts along dimension 0, may hold values from 0 to 15; in each aligned block of 4096 rows (0 to 4095, 4096 to 8191, ...) at most 384 rows name the same one
- local: int32 [8192], P('parts'), parts along dimension 0, may hold values from 0 to 1023
- table_id: int32 [8192], P('parts'), parts along dimension 0, may hold values from 0 to 7
- interp: bfloat16 [8, 128, 128], replicated, may hold values from -0.5 to 0.5
- ctf: float32 [16, 8192], P('parts'), parts along dimension 0, may hold values from 0.2 to 1
Outputs:
- new_map: float32 [32768, 256], P(('parts', 'img')), parts along dimension 0
- evidence: float32 [2048], P(('parts', 'img')), parts along dimension 0
The draws below stay inside these ranges and needn't reach their ends.
There are 2 independent parts, one for each index of `parts`. The reference program is written for one: setup_inputs(seed, part) draws one part's arguments, and reference() takes and returns one part's arrays. A program takes and returns all parts, laid end to end along the dimension named above; an argument that names none is the same for every part. Nothing has to cross between parts.
Inputs may be any that keep to these rules, and one draw needn't show every extreme that they name: `owner`: no slab is named by more than 384 slice blocks, a bound that some block reaches.
All inputs are finite; a program needn't handle non-finite values.
Results may differ from the reference program's by a relative error of at most 0.012.
The reference program's roundings to bfloat16 on the way (of `slices`, `rotated`, `weighted` and `weights`) count: a program that leaves them out, or rounds other values in their place, can miss the bound.
Values may be sent and summed in bfloat16 or wider, within the bound.
A program may use at most 128 MiB of HBM per device.

```python
import math
import jax
import jax.numpy as jnp
import numpy as np
from jax import lax

BW = 128
KB = 64
R = 64
S = 9
G = 8
NT = 8
IMG_DEV = 64
VB_DEV = 1024
IMAGES = 1024
NV = 16384
RB = 4096
MOST = 384
N_IMG = 16


def draw_images(key, part):
    first_key = jax.random.fold_in(jax.random.fold_in(key, 11), 0)
    return jnp.clip(jax.random.normal(first_key, (IMAGES, KB * 2 * BW), jnp.float32), -6.0, 6.0).astype(jnp.bfloat16)


def set_ends(array, own_key, low, high):
    longest = array.shape.index(max(array.shape))
    spots = []
    for shift in (0, 1):
        where = [jax.random.randint(jax.random.fold_in(own_key, axis), (), 0, length) for axis, length in enumerate(array.shape)]
        where[longest] = (where[longest] + shift) % array.shape[longest]
        spots.append(tuple(where))
    return array.at[spots[0]].set(low).at[spots[1]].set(high)


def block_scale(rng, extent, cuts, low, high):
    level, own = 1.0, jax.random.fold_in(rng, 6)
    for dim, parts in cuts:
        draws = jnp.exp(jax.random.uniform(jax.random.fold_in(own, dim), (parts,), jnp.float32, low / len(cuts), high / len(cuts)))
        level = level * jnp.repeat(draws, extent[dim] // parts).reshape([-1 if axis == dim else 1 for axis in range(len(extent))])
    return level


def assign_block(stream_key, own, number, rows, number_of, top, bound, skew):
    order = jax.random.permutation(stream_key, number_of)
    heavy_load, ordinary = shares(number_of, rows * top, bound, skew, True), shares(number_of, rows * top, bound, skew, False)
    places = jnp.arange(number_of)

    def named(lengths, turn):
        used = int((lengths > 0).sum())
        fixed = max(1, used // 4)
        moved = fixed + (places - fixed + turn * (used - fixed)) % max(1, number_of - fixed)
        return jnp.zeros((number_of,), jnp.int32).at[order[jnp.where(places < fixed, places, moved)]].set(jnp.asarray(lengths, jnp.int32))

    lengths = jnp.where(number % 4 == 0, named(heavy_load, number // 4), named(ordinary, number - number // 4 - 1))
    mixed = jax.random.permutation(jax.random.fold_in(own, 3), number_of)
    source_of, taker = mixed[0:number_of // 2 * 2:2], mixed[1:number_of // 2 * 2:2]
    margin = jnp.minimum(lengths[source_of] - 1, bound - lengths[taker]) // 2
    margin = jnp.where((source_of == order[0]) | (taker == order[0]) | (lengths[taker] == 0), 0, jnp.maximum(margin, 0))
    moved = jax.random.randint(jax.random.fold_in(own, 4), (number_of // 2,), 0, 1 << 20) % (margin + 1)
    lengths = lengths.at[source_of].add(-moved).at[taker].add(moved)
    labels = jnp.searchsorted(jnp.cumsum(lengths), jnp.arange(rows * top), side="right").astype(jnp.int32)
    listing = labels.reshape(top, rows).T
    listing = listing[jax.random.permutation(jax.random.fold_in(own, 1), rows)]
    turn = jax.random.randint(jax.random.fold_in(own, 2), (rows, 1), 0, top)
    return jnp.take_along_axis(listing, (jnp.arange(top)[None, :] + turn) % top, axis=1)


def shares(count, total, reach, lean, full):
    loads = [(1 << 20) // math.isqrt(standing ** lean) + 1 for standing in range(1, count + 1)]
    largest = reach if full else min(reach, max(-(-total // count), total * loads[0] // sum(loads)))
    least = 1 if total - largest >= count - 1 else 0
    counts, surplus = [largest] + [least] * (count - 1), total - largest - least * (count - 1)
    while surplus > 0:
        movable = [i for i in range(1, count) if counts[i] < largest] or [i for i in range(1, count) if counts[i] < reach]
        whole, left = sum([loads[i] for i in movable]), surplus
        for i in movable:
            extra = min(reach - counts[i], max(1, left * loads[i] // whole), surplus)
            counts[i] = counts[i] + extra
            surplus = surplus - extra
    return np.array(counts)


def gaussian(own_key, shape, deviation, most, cuts=(), dtype=jnp.bfloat16):
    gain = block_scale(own_key, shape, cuts, -0.22, 0.18) if cuts else 1.0
    drawn = jax.random.normal(own_key, shape, jnp.float32) * deviation * gain
    return jnp.minimum(jnp.maximum(drawn, -most), most).astype(dtype)


def setup_inputs(seed: int = 0, part: int = 0) -> dict:
    key_list = jax.random.split(jax.random.key(seed), 10)
    own_keys = jax.random.split(jax.random.fold_in(key_list[9], part), 10)
    images = draw_images(jax.random.fold_in(jax.random.fold_in(key_list[9], part), 71), part)
    groups = set_ends(jax.random.randint(own_keys[1], (IMAGES,), 0, G), jax.random.fold_in(own_keys[1], 1), 0, G - 1).astype(jnp.int32)
    shifts = set_ends(jax.random.randint(own_keys[2], (S, 2), -3, 4), jax.random.fold_in(own_keys[2], 1), -3, 3).astype(jnp.int32)
    volume = gaussian(own_keys[3], (NV, 2 * BW), 1.0, 6.0, ((0, 16),))
    owner_keys = jax.random.split(jax.random.fold_in(own_keys[4], 1), RB // RB)
    owner_turns = jax.random.permutation(jax.random.fold_in(own_keys[4], 3), RB // RB)
    owner = jax.vmap(lambda own, number: assign_block(jax.random.fold_in(own_keys[4], 2), own, number, RB, N_IMG, 1, MOST, 0))(owner_keys, owner_turns).reshape((RB, 1))
    local = set_ends(jax.random.randint(own_keys[5], (RB,), 0, VB_DEV), jax.random.fold_in(own_keys[5], 1), 0, VB_DEV - 1).astype(jnp.int32)
    table_id = set_ends(jax.random.randint(own_keys[6], (RB,), 0, NT), jax.random.fold_in(own_keys[6], 1), 0, NT - 1).astype(jnp.int32)
    interp = gaussian(key_list[7], (NT, BW, BW), BW ** -0.5, 0.5)
    ctf = jnp.clip(jax.random.uniform(own_keys[8], (G, KB * BW), jnp.float32, 0.2, 1.0), 0.2, 1.0)
    return {"images": images, "groups": groups, "shifts": shifts, "volume": volume, "owner": owner, "local": local, "table_id": table_id, "interp": interp, "ctf": ctf}


exact_mode = lax.Precision.HIGHEST

def phases(shifts):
    freq_x = (jnp.arange(BW) - BW // 2).astype(jnp.float32)
    freq_y = jnp.arange(KB).astype(jnp.float32)
    shift_x = shifts[:, 0].astype(jnp.float32)
    shift_y = shifts[:, 1].astype(jnp.float32)
    angles = 2.0 * math.pi / BW * (shift_x[:, None, None] * freq_x[None, None, :] + shift_y[:, None, None] * freq_y[None, :, None])
    return (jnp.cos(angles), jnp.sin(angles))

def pick_table(blocks_in, table_ids, interp, adjoint):
    tables = interp.astype(jnp.float32)
    if adjoint:
        expanded = jnp.einsum('ncj,tjv->ntcv', blocks_in, tables, precision=exact_mode)
    else:
        expanded = jnp.einsum('ncv,tjv->ntcj', blocks_in, tables, precision=exact_mode)
    one_hot = (table_ids[:, None] == jnp.arange(interp.shape[0])[None, :]).astype(jnp.float32)
    return lax.optimization_barrier(jnp.sum(expanded * one_hot[:, :, None, None], axis=1))

def score_images(image_rows, group_ids, slices, shifts, ctf):
    refs = slices.shape[0]
    count = image_rows.shape[0]
    cosine, sine_values = phases(shifts)
    slice_values = slices.astype(jnp.float32)
    powers = (slice_values[:, :, 0] ** 2 + slice_values[:, :, 1] ** 2).reshape(refs, KB * BW)
    norm_terms = jnp.dot(ctf * ctf, powers.T, precision=exact_mode)
    one_hot = (group_ids[:, None] == jnp.arange(ctf.shape[0])[None, :]).astype(jnp.float32)
    image_ctf = jnp.dot(one_hot, ctf, precision=exact_mode).reshape(count, KB, 1, BW)
    weighted = (image_rows.astype(jnp.float32).reshape(count, KB, 2, BW) * image_ctf).astype(jnp.bfloat16).reshape(count, KB * 2 * BW)
    image_norms = jnp.dot(one_hot, norm_terms, precision=exact_mode)
    scale_factor = 1.0 / math.sqrt(KB * BW)
    score_list = []
    for number in range(cosine.shape[0]):
        real_part = slice_values[:, :, 0] * cosine[number] - slice_values[:, :, 1] * sine_values[number]
        imag_part = slice_values[:, :, 0] * sine_values[number] + slice_values[:, :, 1] * cosine[number]
        rotated = jnp.stack([real_part, imag_part], axis=2).astype(jnp.bfloat16).reshape(refs, KB * 2 * BW)
        intersection = lax.dot_general(weighted, rotated, (((1,), (1,)), ((), ())), preferred_element_type=jnp.float32)
        score_list.append((intersection - 0.5 * image_norms) * scale_factor)
    scores = jnp.stack(score_list, axis=1)
    maximum = lax.optimization_barrier(jnp.max(scores, axis=(1, 2)))
    exponent = jnp.exp(scores - maximum[:, None, None])
    summed = lax.optimization_barrier(jnp.sum(exponent, axis=(1, 2)))
    evidence = maximum + jnp.log(summed)
    weights = (exponent / summed[:, None, None]).astype(jnp.bfloat16)
    accumulated = jnp.zeros((refs, KB, 2, BW), jnp.float32)
    for number in range(cosine.shape[0]):
        partial_sum = lax.dot_general(weights[:, number, :], weighted, (((0,), (0,)), ((), ())), preferred_element_type=jnp.float32).reshape(refs, KB, 2, BW)
        back_real = partial_sum[:, :, 0] * cosine[number] + partial_sum[:, :, 1] * sine_values[number]
        back_imag = partial_sum[:, :, 1] * cosine[number] - partial_sum[:, :, 0] * sine_values[number]
        accumulated = accumulated + jnp.stack([back_real, back_imag], axis=2)
    return (accumulated, evidence)

def reference(images, groups, shifts, volume, owner, local, table_id, interp, ctf):
    volume_index = (owner[:, 0] * VB_DEV + local).astype(jnp.int32)
    volume_rows = volume[volume_index].astype(jnp.float32).reshape(RB, 2, BW)
    slices = pick_table(volume_rows, table_id, interp, False).astype(jnp.bfloat16).reshape(R, KB, 2, BW)

    def image_block(carried, inputs):
        image_rows, group_ids = inputs
        accumulated, evidence = score_images(image_rows, group_ids, slices, shifts, ctf)
        return (carried + accumulated, evidence)
    start = jnp.zeros((R, KB, 2, BW), jnp.float32)
    sums, evidence = lax.scan(image_block, start, (images.reshape(N_IMG, IMG_DEV, KB * 2 * BW), groups.reshape(N_IMG, IMG_DEV)))
    contrib = pick_table(sums.reshape(RB, 2, BW), table_id, interp, True).reshape(RB, 2 * BW)
    new_map = volume.astype(jnp.float32).at[volume_index].add(contrib)
    return (new_map, evidence.reshape(IMAGES))
```

```python
import functools
import math

import jax
import jax.numpy as jnp
from jax import lax
from jax.experimental import pallas as pl
from jax.experimental.pallas import tpu as pltpu
from jax.sharding import PartitionSpec as P

BW = 128
KB = 64
R = 64
GROUP = 4

exact_mode = lax.Precision.HIGHEST
VMEM = pltpu.VMEM


def phases(shifts):
    freq_x = (jnp.arange(BW) - BW // 2).astype(jnp.float32)
    freq_y = jnp.arange(KB).astype(jnp.float32)
    shift_x = shifts[:, 0].astype(jnp.float32)
    shift_y = shifts[:, 1].astype(jnp.float32)
    angles = (
        2.0
        * math.pi
        / BW
        * (
            shift_x[None, :, None] * freq_x[None, None, :]
            + shift_y[None, :, None] * freq_y[:, None, None]
        )
    )
    return (jnp.cos(angles), jnp.sin(angles))


def thirds(x):
    high = x.astype(jnp.bfloat16)
    rest = x - high.astype(jnp.float32)
    mid = rest.astype(jnp.bfloat16)
    low = (rest - mid.astype(jnp.float32)).astype(jnp.bfloat16)
    return (high, mid, low)


def prep_kernel(local_ref, table_ref, volume_ref, interp_ref, out_ref):
    count = local_ref.shape[0]
    blocks = volume_ref.shape[0]
    hot = (
        (local_ref[...] == lax.broadcasted_iota(jnp.int32, (count, blocks), 1))
        .astype(jnp.float32)
        .astype(jnp.bfloat16)
    )
    rows = jnp.dot(hot, volume_ref[...], preferred_element_type=jnp.float32).astype(jnp.bfloat16)
    table = table_ref[...]
    for part in range(2):
        piece = rows[:, part * BW : (part + 1) * BW]
        total = jnp.zeros((count, BW), jnp.float32)
        for t in range(interp_ref.shape[0]):
            value = lax.dot_general(
                piece, interp_ref[t], (((1,), (1,)), ((), ())), preferred_element_type=jnp.float32
            )
            total = jnp.where(table == t, value, total)
        out_ref[:, part * BW : (part + 1) * BW] = total.astype(jnp.bfloat16)


def end_kernel(local_ref, table_ref, real_ref, imag_ref, volume_ref, interp_ref, out_ref):
    count = table_ref.shape[0]
    blocks = volume_ref.shape[0]
    hot = (
        (local_ref[...] == lax.broadcasted_iota(jnp.int32, (blocks, count), 0))
        .astype(jnp.float32)
        .astype(jnp.bfloat16)
    )
    table = table_ref[...]
    for part, received_ref in enumerate((real_ref, imag_ref)):
        cols = slice(part * BW, (part + 1) * BW)
        total = jnp.zeros((count, BW), jnp.float32)
        pieces = thirds(received_ref[...])
        for t in range(interp_ref.shape[0]):
            value = jnp.zeros((count, BW), jnp.float32)
            for piece in pieces[::-1]:
                value = value + jnp.dot(
                    piece, interp_ref[t], preferred_element_type=jnp.float32
                )
            total = jnp.where(table == t, value, total)
        added = jnp.zeros((blocks, BW), jnp.float32)
        for piece in thirds(total)[::-1]:
            added = added + jnp.dot(hot, piece, preferred_element_type=jnp.float32)
        out_ref[:, cols] = volume_ref[:, cols].astype(jnp.float32) + added


def weight_kernel(images_ref, hot_ref, ctf_ref, out_ref):
    values = jnp.dot(
        hot_ref[...], ctf_ref[...], precision=exact_mode, preferred_element_type=jnp.float32
    )
    for k in range(ctf_ref.shape[1] // BW):
        factor = values[:, k * BW : (k + 1) * BW]
        for part in range(2):
            cols = slice((2 * k + part) * BW, (2 * k + part + 1) * BW)
            out_ref[:, cols] = (images_ref[:, cols].astype(jnp.float32) * factor).astype(
                jnp.bfloat16
            )


def main_kernel(
    target_ref,
    gathered_ref,
    weighted_ref,
    hot_ref,
    ctf_ref,
    cos_ref,
    sin_ref,
    out_real,
    out_imag,
    evidence_ref,
    wide,
    real_rows,
    imag_rows,
    powers,
    rotated,
    scores,
    weights,
):
    shifts = cos_ref.shape[1]
    count = weighted_ref.shape[0]
    slots = gathered_ref.shape[0]
    step = 256

    @pl.loop(0, slots // step)
    def _(i):
        rows = pl.ds(pl.multiple_of(i * step, step), step)
        wide[rows, :] = gathered_ref[rows, :].astype(jnp.float32)
        out_real[rows, :] = jnp.zeros((step, BW), jnp.float32)
        out_imag[rows, :] = jnp.zeros((step, BW), jnp.float32)

    scores[...] = jnp.zeros_like(scores)

    @pl.loop(0, KB // GROUP)
    def _(i):
        for k in range(GROUP):
            b = i * GROUP + k
            for r in range(R):
                row = wide[pl.ds(target_ref[r * KB + b], 1), :]
                real_rows[k, r : r + 1, :] = row[:, :BW]
                imag_rows[k, r : r + 1, :] = row[:, BW:]
        for k in range(GROUP):
            b = i * GROUP + k
            real = real_rows[k]
            imag = imag_rows[k]
            powers[:, pl.ds(pl.multiple_of(b * BW, BW), BW)] = real * real + imag * imag
            for s in range(shifts):
                c = cos_ref[b, s : s + 1, :]
                n = sin_ref[b, s : s + 1, :]
                rows = slice(s * R, (s + 1) * R)
                rotated[rows, 2 * k * BW : (2 * k + 1) * BW] = (real * c - imag * n).astype(
                    jnp.bfloat16
                )
                rotated[rows, (2 * k + 1) * BW : (2 * k + 2) * BW] = (
                    real * n + imag * c
                ).astype(jnp.bfloat16)
        width = GROUP * 2 * BW
        part = weighted_ref[:, pl.ds(pl.multiple_of(i * width, width), width)]
        scores[...] += lax.dot_general(
            rotated[...], part, (((1,), (1,)), ((), ())), preferred_element_type=jnp.float32
        )

    ctf = ctf_ref[...]
    norms = lax.dot_general(
        powers[...],
        ctf * ctf,
        (((1,), (1,)), ((), ())),
        precision=exact_mode,
        preferred_element_type=jnp.float32,
    )
    image_norms = lax.dot_general(
        norms,
        hot_ref[...],
        (((1,), (1,)), ((), ())),
        precision=exact_mode,
        preferred_element_type=jnp.float32,
    )
    scale = 1.0 / math.sqrt(KB * BW)
    values = (scores[...].reshape(shifts, R, count) - 0.5 * image_norms[None]) * scale
    most = jnp.max(jnp.max(values, axis=0), axis=0, keepdims=True)
    exponent = jnp.exp(values - most[None])
    summed = jnp.sum(jnp.sum(exponent, axis=0), axis=0, keepdims=True)
    evidence_ref[...] = most + jnp.log(summed)
    weights[...] = (exponent / summed[None]).astype(jnp.bfloat16).reshape(shifts * R, count)

    @pl.loop(0, KB)
    def _(b):
        part = weighted_ref[:, pl.ds(pl.multiple_of(b * 2 * BW, 2 * BW), 2 * BW)]
        real = jnp.zeros((R, BW), jnp.float32)
        imag = jnp.zeros((R, BW), jnp.float32)
        for s in range(shifts):
            product = jnp.dot(
                weights[s * R : (s + 1) * R, :], part, preferred_element_type=jnp.float32
            )
            c = cos_ref[b, s : s + 1, :]
            n = sin_ref[b, s : s + 1, :]
            real = real + product[:, :BW] * c + product[:, BW:] * n
            imag = imag + product[:, BW:] * c - product[:, :BW] * n
        k = lax.rem(b, 2)
        real_rows[k] = real
        imag_rows[k] = imag
        for r in range(R):
            row = pl.ds(target_ref[r * KB + b], 1)
            out_real[row, :] = real_rows[k, r : r + 1, :]
            out_imag[row, :] = imag_rows[k, r : r + 1, :]


def per_device(images, groups, shifts, volume, owner, local, table_id, interp, ctf):
    devices = lax.axis_size("img")
    myself = lax.axis_index("img")
    block_count = R * KB
    count = images.shape[0]
    blocks = volume.shape[0]
    tries = shifts.shape[0]
    capacity = max(2, 3 * block_count // (2 * devices))
    slots = devices * capacity
    owners = owner[:, 0]

    lines = block_count // BW
    member = (owners[:, None] == jnp.arange(devices, dtype=jnp.int32)[None, :]).astype(jnp.bfloat16)
    member = member.reshape(lines, BW, devices)
    lower = jnp.tril(jnp.ones((BW, BW), jnp.bfloat16))
    within = jnp.einsum("ab,kbn->kan", lower, member, preferred_element_type=jnp.float32)
    before = jnp.dot(
        jnp.tril(jnp.ones((lines, lines), jnp.bfloat16), -1),
        within[:, -1, :].astype(jnp.bfloat16),
        preferred_element_type=jnp.float32,
    )
    rank = jnp.sum((within + before[:, None, :]) * member.astype(jnp.float32), axis=2) - 1.0
    position = rank.reshape(block_count).astype(jnp.int32)
    target = owners * capacity + position

    place = jnp.where(owners == myself, position, capacity)
    chosen = (place[None, :] == jnp.arange(capacity, dtype=jnp.int32)[:, None]).astype(jnp.bfloat16)
    columns = jnp.stack([local // 256, local % 256, table_id], axis=1).astype(jnp.bfloat16)
    slot_info = jnp.dot(chosen, columns, preferred_element_type=jnp.float32).astype(jnp.int32)
    slot_local = slot_info[:, 0] * 256 + slot_info[:, 1]
    slot_table = slot_info[:, 2:3]

    own_slices = pl.pallas_call(
        prep_kernel,
        out_shape=jax.ShapeDtypeStruct((capacity, 2 * BW), jnp.bfloat16),
        name="prep",
    )(slot_local[:, None], slot_table, volume, interp)
    gathered = lax.all_gather(own_slices, "img", axis=0, tiled=True)

    hot = (groups[:, None] == jnp.arange(ctf.shape[0])[None, :]).astype(jnp.float32)
    width = 2048
    weighted = pl.pallas_call(
        weight_kernel,
        out_shape=jax.ShapeDtypeStruct(images.shape, jnp.bfloat16),
        grid=(images.shape[1] // width,),
        in_specs=[
            pl.BlockSpec((count, width), lambda i: (0, i)),
            pl.BlockSpec((count, ctf.shape[0]), lambda i: (0, 0)),
            pl.BlockSpec((ctf.shape[0], width // 2), lambda i: (0, i)),
        ],
        out_specs=pl.BlockSpec((count, width), lambda i: (0, i)),
        cost_estimate=pl.CostEstimate(
            flops=20 * images.size, bytes_accessed=12 * images.size, transcendentals=0
        ),
        name="weight",
    )(images, hot, ctf)
    cosine, sine = phases(shifts)

    out_real, out_imag, evidence = pl.pallas_call(
        main_kernel,
        out_shape=(
            jax.ShapeDtypeStruct((slots, BW), jnp.float32),
            jax.ShapeDtypeStruct((slots, BW), jnp.float32),
            jax.ShapeDtypeStruct((1, count), jnp.float32),
        ),
        in_specs=[pl.BlockSpec(memory_space=pltpu.SMEM)]
        + [pl.BlockSpec(memory_space=VMEM)] * 6,
        out_specs=(pl.BlockSpec(memory_space=VMEM),) * 3,
        scratch_shapes=[
            VMEM((slots, 2 * BW), jnp.float32),
            VMEM((GROUP, R, BW), jnp.float32),
            VMEM((GROUP, R, BW), jnp.float32),
            VMEM((R, KB * BW), jnp.float32),
            VMEM((tries * R, GROUP * 2 * BW), jnp.bfloat16),
            VMEM((tries * R, count), jnp.float32),
            VMEM((tries * R, count), jnp.bfloat16),
        ],
        compiler_params=pltpu.CompilerParams(vmem_limit_bytes=48 << 20),
        name="score",
    )(target, gathered, weighted, hot, ctf, cosine, sine)

    received_real = lax.psum_scatter(out_real, "img", scatter_dimension=0, tiled=True)
    received_imag = lax.psum_scatter(out_imag, "img", scatter_dimension=0, tiled=True)
    new_map = pl.pallas_call(
        end_kernel,
        out_shape=jax.ShapeDtypeStruct((blocks, 2 * BW), jnp.float32),
        name="finish",
    )(slot_local[None, :], slot_table, received_real, received_imag, volume, interp)
    return (new_map, evidence.reshape(count))


def solution(mesh):
    return jax.shard_map(
        per_device,
        mesh=mesh,
        in_specs=(
            P(("parts", "img"), None),
            P(("parts", "img")),
            P("parts", None),
            P(("parts", "img"), None),
            P("parts", None),
            P("parts"),
            P("parts"),
            P(),
            P("parts", None),
        ),
        out_specs=(P(("parts", "img"), None), P(("parts", "img"))),
        check_vma=False,
    )
```

```python
import functools
import math

import jax
import jax.numpy as jnp
from jax import lax
from jax.experimental import pallas as pl
from jax.experimental.pallas import tpu as pltpu
from jax.sharding import PartitionSpec as P

BW = 128
KB = 64
R = 64
GROUP = 4

exact_mode = lax.Precision.HIGHEST
VMEM = pltpu.VMEM


def phases(shifts):
    freq_x = (jnp.arange(BW) - BW // 2).astype(jnp.float32)
    freq_y = jnp.arange(KB).astype(jnp.float32)
    shift_x = shifts[:, 0].astype(jnp.float32)
    shift_y = shifts[:, 1].astype(jnp.float32)
    angles = (
        2.0
        * math.pi
        / BW
        * (
            shift_x[None, :, None] * freq_x[None, None, :]
            + shift_y[None, :, None] * freq_y[:, None, None]
        )
    )
    return (jnp.cos(angles), jnp.sin(angles))


def thirds(x):
    high = x.astype(jnp.bfloat16)
    rest = x - high.astype(jnp.float32)
    mid = rest.astype(jnp.bfloat16)
    low = (rest - mid.astype(jnp.float32)).astype(jnp.bfloat16)
    return (high, mid, low)


def prep_kernel(local_ref, table_ref, volume_ref, interp_ref, out_ref):
    count = local_ref.shape[0]
    blocks = volume_ref.shape[0]
    hot = (
        (local_ref[...] == lax.broadcasted_iota(jnp.int32, (count, blocks), 1))
        .astype(jnp.float32)
        .astype(jnp.bfloat16)
    )
    rows = jnp.dot(hot, volume_ref[...], preferred_element_type=jnp.float32).astype(jnp.bfloat16)
    table = table_ref[...]
    for part in range(2):
        piece = rows[:, part * BW : (part + 1) * BW]
        total = jnp.zeros((count, BW), jnp.float32)
        for t in range(interp_ref.shape[0]):
            value = lax.dot_general(
                piece, interp_ref[t], (((1,), (1,)), ((), ())), preferred_element_type=jnp.float32
            )
            total = jnp.where(table == t, value, total)
        out_ref[:, part * BW : (part + 1) * BW] = total.astype(jnp.bfloat16)


def end_kernel(local_ref, table_ref, real_ref, imag_ref, volume_ref, interp_ref, out_ref):
    count = table_ref.shape[0]
    blocks = volume_ref.shape[0]
    hot = (
        (local_ref[...] == lax.broadcasted_iota(jnp.int32, (blocks, count), 0))
        .astype(jnp.float32)
        .astype(jnp.bfloat16)
    )
    table = table_ref[...]
    for part, received_ref in enumerate((real_ref, imag_ref)):
        cols = slice(part * BW, (part + 1) * BW)
        total = jnp.zeros((count, BW), jnp.float32)
        pieces = thirds(received_ref[...])
        for t in range(interp_ref.shape[0]):
            value = jnp.zeros((count, BW), jnp.float32)
            for piece in pieces[::-1]:
                value = value + jnp.dot(
                    piece, interp_ref[t], preferred_element_type=jnp.float32
                )
            total = jnp.where(table == t, value, total)
        added = jnp.zeros((blocks, BW), jnp.float32)
        for piece in thirds(total)[::-1]:
            added = added + jnp.dot(hot, piece, preferred_element_type=jnp.float32)
        out_ref[:, cols] = volume_ref[:, cols].astype(jnp.float32) + added


def weight_kernel(images_ref, hot_ref, ctf_ref, out_ref):
    values = jnp.dot(
        hot_ref[...], ctf_ref[...], precision=exact_mode, preferred_element_type=jnp.float32
    )
    for k in range(ctf_ref.shape[1] // BW):
        factor = values[:, k * BW : (k + 1) * BW]
        for part in range(2):
            cols = slice((2 * k + part) * BW, (2 * k + part + 1) * BW)
            out_ref[:, cols] = (images_ref[:, cols].astype(jnp.float32) * factor).astype(
                jnp.bfloat16
            )


def main_kernel(
    target_ref,
    gathered_ref,
    weighted_ref,
    hot_ref,
    ctf_ref,
    cos_ref,
    sin_ref,
    out_real,
    out_imag,
    evidence_ref,
    wide,
    real_rows,
    imag_rows,
    powers,
    rotated,
    scores,
    weights,
):
    shifts = cos_ref.shape[1]
    count = weighted_ref.shape[0]
    slots = gathered_ref.shape[0]
    step = 256

    @pl.loop(0, slots // step)
    def _(i):
        rows = pl.ds(pl.multiple_of(i * step, step), step)
        wide[rows, :] = gathered_ref[rows, :].astype(jnp.float32)
        out_real[rows, :] = jnp.zeros((step, BW), jnp.float32)
        out_imag[rows, :] = jnp.zeros((step, BW), jnp.float32)

    scores[...] = jnp.zeros_like(scores)

    @pl.loop(0, KB // GROUP)
    def _(i):
        for k in range(GROUP):
            b = i * GROUP + k
            for r in range(R):
                row = wide[pl.ds(target_ref[r * KB + b], 1), :]
                real_rows[k, r : r + 1, :] = row[:, :BW]
                imag_rows[k, r : r + 1, :] = row[:, BW:]
        for k in range(GROUP):
            b = i * GROUP + k
            real = real_rows[k]
            imag = imag_rows[k]
            powers[:, pl.ds(pl.multiple_of(b * BW, BW), BW)] = real * real + imag * imag
            for s in range(shifts):
                c = cos_ref[b, s : s + 1, :]
                n = sin_ref[b, s : s + 1, :]
                rows = slice(s * R, (s + 1) * R)
                rotated[rows, 2 * k * BW : (2 * k + 1) * BW] = (real * c - imag * n).astype(
                    jnp.bfloat16
                )
                rotated[rows, (2 * k + 1) * BW : (2 * k + 2) * BW] = (
                    real * n + imag * c
                ).astype(jnp.bfloat16)
        width = GROUP * 2 * BW
        part = weighted_ref[:, pl.ds(pl.multiple_of(i * width, width), width)]
        scores[...] += lax.dot_general(
            rotated[...], part, (((1,), (1,)), ((), ())), preferred_element_type=jnp.float32
        )

    ctf = ctf_ref[...]
    norms = lax.dot_general(
        powers[...],
        ctf * ctf,
        (((1,), (1,)), ((), ())),
        precision=exact_mode,
        preferred_element_type=jnp.float32,
    )
    image_norms = lax.dot_general(
        norms,
        hot_ref[...],
        (((1,), (1,)), ((), ())),
        precision=exact_mode,
        preferred_element_type=jnp.float32,
    )
    scale = 1.0 / math.sqrt(KB * BW)
    values = (scores[...].reshape(shifts, R, count) - 0.5 * image_norms[None]) * scale
    most = jnp.max(jnp.max(values, axis=0), axis=0, keepdims=True)
    exponent = jnp.exp(values - most[None])
    summed = jnp.sum(jnp.sum(exponent, axis=0), axis=0, keepdims=True)
    evidence_ref[...] = most + jnp.log(summed)
    weights[...] = (exponent / summed[None]).astype(jnp.bfloat16).reshape(shifts * R, count)

    @pl.loop(0, KB)
    def _(b):
        part = weighted_ref[:, pl.ds(pl.multiple_of(b * 2 * BW, 2 * BW), 2 * BW)]
        real = jnp.zeros((R, BW), jnp.float32)
        imag = jnp.zeros((R, BW), jnp.float32)
        for s in range(shifts):
            product = jnp.dot(
                weights[s * R : (s + 1) * R, :], part, preferred_element_type=jnp.float32
            )
            c = cos_ref[b, s : s + 1, :]
            n = sin_ref[b, s : s + 1, :]
            real = real + product[:, :BW] * c + product[:, BW:] * n
            imag = imag + product[:, BW:] * c - product[:, :BW] * n
        k = lax.rem(b, 2)
        real_rows[k] = real
        imag_rows[k] = imag
        for r in range(R):
            row = pl.ds(target_ref[r * KB + b], 1)
            out_real[row, :] = real_rows[k, r : r + 1, :]
            out_imag[row, :] = imag_rows[k, r : r + 1, :]


def split_axes(devices):
    pairs = devices // 2
    middle = 1
    while 4 * middle * middle <= pairs:
        middle *= 2
    return pairs // middle, middle


def place_of(devices):
    outer, middle = split_axes(devices)
    me = lax.axis_index("img")
    return outer, middle, me // (2 * middle), (me // 2) % middle, me % 2


def greet(outer, middle, a, b, c, device):
    barrier = pltpu.get_barrier_semaphore()
    peers = [device((a + d) % outer, b, c) for d in range(1, outer)]
    peers += [device(a, (b + d) % middle, c) for d in range(1, middle)]
    peers += [device(a, b, 1 - c)]
    for peer in peers:
        pl.semaphore_signal(
            barrier, inc=1, device_id={"img": peer}, device_id_type=pl.DeviceIdType.MESH
        )
    pl.semaphore_wait(barrier, len(peers))


def spread_kernel(devices, own_ref, out_ref, sem_a, sem_b, sem_c, sem_own):
    outer, middle, a, b, c = place_of(devices)

    def device(a, b, c):
        return (a * middle + b) * 2 + c

    def slot(a, b, c):
        return (c * middle + b) * outer + a

    def send(src, where, sems, peer):
        copy = pltpu.make_async_remote_copy(
            src_ref=src,
            dst_ref=out_ref.at[where],
            send_sem=sems[0],
            recv_sem=sems[1],
            device_id={"img": peer},
            device_id_type=pl.DeviceIdType.MESH,
        )
        copy.start()
        return copy

    greet(outer, middle, a, b, c, device)
    keep = pltpu.make_async_copy(own_ref, out_ref.at[slot(a, b, c)], sem_own)
    keep.start()
    first, second, third = {}, {}, {}

    def to_core(da, db):
        where = slot((a - da + outer) % outer, (b - db + middle) % middle, c)
        src = own_ref if da == 0 and db == 0 else out_ref.at[where]
        sems = (sem_c.at[0, da, db], sem_c.at[1, da, db])
        third[da, db] = send(src, where, sems, device(a, b, 1 - c))

    def to_middle(da):
        where = slot((a - da + outer) % outer, b, c)
        src = own_ref if da == 0 else out_ref.at[where]
        for db in range(1, middle):
            sems = (sem_b.at[0, da, db], sem_b.at[1, da, db])
            second[da, db] = send(src, where, sems, device(a, (b + db) % middle, c))

    here = slot(a, b, c)
    to_middle(0)
    for d in range(1, outer):
        first[d] = send(
            own_ref, here, (sem_a.at[0, d], sem_a.at[1, d]), device((a + d) % outer, b, c)
        )
    to_core(0, 0)
    for db in range(1, middle):
        second[0, db].wait_recv()
        to_core(0, db)
    for d in sorted(range(1, outer), key=lambda d: min(d, outer - d)):
        first[d].wait_recv()
        to_middle(d)
        to_core(d, 0)
    for d in range(1, outer):
        for db in range(1, middle):
            second[d, db].wait_recv()
            to_core(d, db)
    keep.wait()
    for copy in list(first.values()) + list(second.values()):
        copy.wait_send()
    for copy in third.values():
        copy.wait()


def collect_kernel(
    devices,
    real_ref,
    imag_ref,
    out_real,
    out_imag,
    core_box,
    middle_out,
    middle_box,
    outer_out,
    outer_box,
    sem_c,
    sem_b,
    sem_a,
):
    outer, middle, a, b, c = place_of(devices)
    inputs = (real_ref, imag_ref)

    def device(a, b, c):
        return (a * middle + b) * 2 + c

    def send(src, dst, sems, peer):
        copy = pltpu.make_async_remote_copy(
            src_ref=src,
            dst_ref=dst,
            send_sem=sems[0],
            recv_sem=sems[1],
            device_id={"img": peer},
            device_id_type=pl.DeviceIdType.MESH,
        )
        copy.start()
        return copy

    greet(outer, middle, a, b, c, device)
    order = list(range(1, middle)) + [0]
    first, second, third = {}, {}, {}
    for db in order:
        bq = (b + db) % middle
        for part in range(2):
            first[db, part] = send(
                inputs[part].at[1 - c, bq],
                core_box.at[db, part],
                (sem_c.at[0, db, part], sem_c.at[1, db, part]),
                device(a, b, 1 - c),
            )

    def pair_sum(db, da, part):
        bq = (b + db) % middle
        aq = (a + da) % outer
        return inputs[part][c, bq, aq] + core_box[db, part, aq]

    steps = list(range(1, outer)) + [0]
    for db in range(1, middle):
        first[db, 0].wait_recv()
        first[db, 1].wait_recv()
        for da in steps:
            for part in range(2):
                middle_out[db - 1, da, part] = pair_sum(db, da, part).astype(jnp.bfloat16)
            second[db, da] = send(
                middle_out.at[db - 1, da],
                middle_box.at[db - 1, da],
                (sem_b.at[0, db, da], sem_b.at[1, db, da]),
                device(a, (b + db) % middle, c),
            )
    first[0, 0].wait_recv()
    first[0, 1].wait_recv()
    outs = (out_real, out_imag)
    for da in steps:
        for db in range(1, middle):
            second[db, da].wait_recv()
        for part in range(2):
            total = pair_sum(0, da, part)
            for db in range(1, middle):
                total = total + middle_box[db - 1, da, part].astype(jnp.float32)
            if da:
                outer_out[da - 1, part] = total.astype(jnp.bfloat16)
            else:
                outs[part][...] = total
        if da:
            third[da] = send(
                outer_out.at[da - 1],
                outer_box.at[da - 1],
                (sem_a.at[0, da], sem_a.at[1, da]),
                device((a + da) % outer, b, c),
            )
    for da in range(1, outer):
        third[da].wait_recv()
        for part in range(2):
            outs[part][...] += outer_box[da - 1, part].astype(jnp.float32)
    for copy in list(first.values()) + list(second.values()) + list(third.values()):
        copy.wait_send()


def spread(own, devices):
    outer, middle = split_axes(devices)
    return pl.pallas_call(
        functools.partial(spread_kernel, devices),
        out_shape=jax.ShapeDtypeStruct((devices,) + own.shape, own.dtype),
        in_specs=[pl.BlockSpec(memory_space=VMEM)],
        out_specs=pl.BlockSpec(memory_space=VMEM),
        scratch_shapes=[
            pltpu.SemaphoreType.DMA((2, outer)),
            pltpu.SemaphoreType.DMA((2, outer, middle)),
            pltpu.SemaphoreType.DMA((2, outer, middle)),
            pltpu.SemaphoreType.DMA,
        ],
        compiler_params=pltpu.CompilerParams(
            collective_id=0, has_side_effects=True, vmem_limit_bytes=16 << 20
        ),
        name="spread",
    )(own)


def collect(real, imag, devices, capacity):
    outer, middle = split_axes(devices)
    shape = (2, middle, outer, capacity, BW)
    most = max(1, middle - 1)
    return pl.pallas_call(
        functools.partial(collect_kernel, devices),
        out_shape=(jax.ShapeDtypeStruct((capacity, BW), jnp.float32),) * 2,
        in_specs=[pl.BlockSpec(memory_space=VMEM)] * 2,
        out_specs=(pl.BlockSpec(memory_space=VMEM),) * 2,
        scratch_shapes=[
            VMEM((middle, 2, outer, capacity, BW), jnp.float32),
            VMEM((most, outer, 2, capacity, BW), jnp.bfloat16),
            VMEM((most, outer, 2, capacity, BW), jnp.bfloat16),
            VMEM((max(1, outer - 1), 2, capacity, BW), jnp.bfloat16),
            VMEM((max(1, outer - 1), 2, capacity, BW), jnp.bfloat16),
            pltpu.SemaphoreType.DMA((2, middle, 2)),
            pltpu.SemaphoreType.DMA((2, middle, outer)),
            pltpu.SemaphoreType.DMA((2, outer)),
        ],
        compiler_params=pltpu.CompilerParams(
            collective_id=1, has_side_effects=True, vmem_limit_bytes=40 << 20
        ),
        name="collect",
    )(real.reshape(shape), imag.reshape(shape))


def per_device(images, groups, shifts, volume, owner, local, table_id, interp, ctf):
    devices = lax.axis_size("img")
    myself = lax.axis_index("img")
    block_count = R * KB
    count = images.shape[0]
    blocks = volume.shape[0]
    tries = shifts.shape[0]
    capacity = max(2, 3 * block_count // (2 * devices))
    slots = devices * capacity
    owners = owner[:, 0]

    lines = block_count // BW
    member = (owners[:, None] == jnp.arange(devices, dtype=jnp.int32)[None, :]).astype(jnp.bfloat16)
    member = member.reshape(lines, BW, devices)
    lower = jnp.tril(jnp.ones((BW, BW), jnp.bfloat16))
    within = jnp.einsum("ab,kbn->kan", lower, member, preferred_element_type=jnp.float32)
    before = jnp.dot(
        jnp.tril(jnp.ones((lines, lines), jnp.bfloat16), -1),
        within[:, -1, :].astype(jnp.bfloat16),
        preferred_element_type=jnp.float32,
    )
    rank = jnp.sum((within + before[:, None, :]) * member.astype(jnp.float32), axis=2) - 1.0
    position = rank.reshape(block_count).astype(jnp.int32)
    outer, middle = split_axes(devices)
    ordered = ((owners % 2) * middle + (owners // 2) % middle) * outer + owners // (2 * middle)
    target = ordered * capacity + position

    place = jnp.where(owners == myself, position, capacity)
    chosen = (place[None, :] == jnp.arange(capacity, dtype=jnp.int32)[:, None]).astype(jnp.bfloat16)
    columns = jnp.stack([local // 256, local % 256, table_id], axis=1).astype(jnp.bfloat16)
    slot_info = jnp.dot(chosen, columns, preferred_element_type=jnp.float32).astype(jnp.int32)
    slot_local = slot_info[:, 0] * 256 + slot_info[:, 1]
    slot_table = slot_info[:, 2:3]

    own_slices = pl.pallas_call(
        prep_kernel,
        out_shape=jax.ShapeDtypeStruct((capacity, 2 * BW), jnp.bfloat16),
        name="prep",
    )(slot_local[:, None], slot_table, volume, interp)
    gathered = spread(own_slices, devices).reshape(slots, 2 * BW)

    hot = (groups[:, None] == jnp.arange(ctf.shape[0])[None, :]).astype(jnp.float32)
    width = 2048
    weighted = pl.pallas_call(
        weight_kernel,
        out_shape=jax.ShapeDtypeStruct(images.shape, jnp.bfloat16),
        grid=(images.shape[1] // width,),
        in_specs=[
            pl.BlockSpec((count, width), lambda i: (0, i)),
            pl.BlockSpec((count, ctf.shape[0]), lambda i: (0, 0)),
            pl.BlockSpec((ctf.shape[0], width // 2), lambda i: (0, i)),
        ],
        out_specs=pl.BlockSpec((count, width), lambda i: (0, i)),
        cost_estimate=pl.CostEstimate(
            flops=20 * images.size, bytes_accessed=12 * images.size, transcendentals=0
        ),
        name="weight",
    )(images, hot, ctf)
    cosine, sine = phases(shifts)

    out_real, out_imag, evidence = pl.pallas_call(
        main_kernel,
        out_shape=(
            jax.ShapeDtypeStruct((slots, BW), jnp.float32),
            jax.ShapeDtypeStruct((slots, BW), jnp.float32),
            jax.ShapeDtypeStruct((1, count), jnp.float32),
        ),
        in_specs=[pl.BlockSpec(memory_space=pltpu.SMEM)]
        + [pl.BlockSpec(memory_space=VMEM)] * 6,
        out_specs=(pl.BlockSpec(memory_space=VMEM),) * 3,
        scratch_shapes=[
            VMEM((slots, 2 * BW), jnp.float32),
            VMEM((GROUP, R, BW), jnp.float32),
            VMEM((GROUP, R, BW), jnp.float32),
            VMEM((R, KB * BW), jnp.float32),
            VMEM((tries * R, GROUP * 2 * BW), jnp.bfloat16),
            VMEM((tries * R, count), jnp.float32),
            VMEM((tries * R, count), jnp.bfloat16),
        ],
        compiler_params=pltpu.CompilerParams(vmem_limit_bytes=48 << 20),
        name="score",
    )(target, gathered, weighted, hot, ctf, cosine, sine)

    received_real, received_imag = collect(out_real, out_imag, devices, capacity)
    new_map = pl.pallas_call(
        end_kernel,
        out_shape=jax.ShapeDtypeStruct((blocks, 2 * BW), jnp.float32),
        name="finish",
    )(slot_local[None, :], slot_table, received_real, received_imag, volume, interp)
    return (new_map, evidence.reshape(count))


def solution(mesh):
    return jax.shard_map(
        per_device,
        mesh=mesh,
        in_specs=(
            P(("parts", "img"), None),
            P(("parts", "img")),
            P("parts", None),
            P(("parts", "img"), None),
            P("parts", None),
            P("parts"),
            P("parts"),
            P(),
            P("parts", None),
        ),
        out_specs=(P(("parts", "img"), None), P(("parts", "img"))),
        check_vma=False,
    )
```

```python
import functools
import math

import jax
import jax.numpy as jnp
from jax import lax
from jax.experimental import pallas as pl
from jax.experimental.pallas import tpu as pltpu
from jax.sharding import PartitionSpec as P

BW = 128
KB = 64
R = 64
GROUP = 4

exact_mode = lax.Precision.HIGHEST
VMEM = pltpu.VMEM


def phases(shifts):
    freq_x = (jnp.arange(BW) - BW // 2).astype(jnp.float32)
    freq_y = jnp.arange(KB).astype(jnp.float32)
    shift_x = shifts[:, 0].astype(jnp.float32)
    shift_y = shifts[:, 1].astype(jnp.float32)
    angles = (
        2.0
        * math.pi
        / BW
        * (
            shift_x[None, :, None] * freq_x[None, None, :]
            + shift_y[None, :, None] * freq_y[:, None, None]
        )
    )
    return (jnp.cos(angles), jnp.sin(angles))


def thirds(x):
    high = x.astype(jnp.bfloat16)
    rest = x - high.astype(jnp.float32)
    mid = rest.astype(jnp.bfloat16)
    low = (rest - mid.astype(jnp.float32)).astype(jnp.bfloat16)
    return (high, mid, low)


def prep_kernel(
    devices, owner_ref, info_ref, volume_ref, interp_ref, out_ref, target_ref, row_ref, table_ref
):
    lines = owner_ref.shape[0]
    count = out_ref.shape[0]
    blocks = volume_ref.shape[0]
    outer, middle = split_axes(devices)
    me = lax.axis_index("img")
    owner = owner_ref[...]
    bits = jnp.bfloat16

    def one(condition):
        return jnp.where(condition, 1.0, 0.0).astype(bits)

    def index(shape, axis):
        return lax.broadcasted_iota(jnp.int32, shape, axis)

    upto = one(index((BW, BW), 0) <= index((BW, BW), 1))
    earlier = one(index((lines, lines), 1) < index((lines, lines), 0))
    every = jnp.ones((BW, BW), bits)
    target = jnp.zeros((lines, BW), jnp.float32)
    for o in range(devices):
        mine = one(owner == o)
        rank = jnp.dot(mine, upto, preferred_element_type=jnp.float32)
        above = jnp.dot(earlier, mine, preferred_element_type=jnp.float32).astype(bits)
        rank = rank + jnp.dot(above, every, preferred_element_type=jnp.float32)
        order = ((o % 2) * middle + (o // 2) % middle) * outer + o // (2 * middle)
        target = jnp.where(owner == o, rank + (order * count - 1.0), target)
    target = target.astype(jnp.int32)
    target_ref[...] = target

    order = ((me % 2) * middle + (me // 2) % middle) * outer + me // (2 * middle)
    place = target - order * count
    slot_rows = jnp.zeros((8, count), jnp.float32)
    slot_columns = jnp.zeros((count, 8), jnp.float32)
    wanted = index((count, BW), 0)
    for k in range(lines):
        chosen = one(place[k : k + 1, :] == wanted)
        info = info_ref[k].astype(jnp.float32).astype(bits)
        dims = (((1,), (1,)), ((), ()))
        slot_rows = slot_rows + lax.dot_general(
            info, chosen, dims, preferred_element_type=jnp.float32
        )
        slot_columns = slot_columns + lax.dot_general(
            chosen, info, dims, preferred_element_type=jnp.float32
        )
    slot_rows = slot_rows.astype(jnp.int32)
    slot_columns = slot_columns.astype(jnp.int32)
    row_ref[...] = slot_rows[0:1] * 256 + slot_rows[1:2]
    local = slot_columns[:, 0:1] * 256 + slot_columns[:, 1:2]
    table = slot_columns[:, 2:3]
    table_ref[...] = table

    hot = one(local == index((count, blocks), 1))
    rows = jnp.dot(hot, volume_ref[...], preferred_element_type=jnp.float32).astype(bits)
    for part in range(2):
        piece = rows[:, part * BW : (part + 1) * BW]
        total = jnp.zeros((count, BW), jnp.float32)
        for t in range(interp_ref.shape[0]):
            value = lax.dot_general(
                piece, interp_ref[t], (((1,), (1,)), ((), ())), preferred_element_type=jnp.float32
            )
            total = jnp.where(table == t, value, total)
        out_ref[:, part * BW : (part + 1) * BW] = total.astype(bits)


def end_kernel(local_ref, table_ref, real_ref, imag_ref, volume_ref, interp_ref, out_ref):
    count = table_ref.shape[0]
    blocks = volume_ref.shape[0]
    hot = (
        (local_ref[...] == lax.broadcasted_iota(jnp.int32, (blocks, count), 0))
        .astype(jnp.float32)
        .astype(jnp.bfloat16)
    )
    table = table_ref[...]
    for part, received_ref in enumerate((real_ref, imag_ref)):
        cols = slice(part * BW, (part + 1) * BW)
        total = jnp.zeros((count, BW), jnp.float32)
        pieces = thirds(received_ref[...])[:2]
        for t in range(interp_ref.shape[0]):
            value = jnp.zeros((count, BW), jnp.float32)
            for piece in pieces[::-1]:
                value = value + jnp.dot(
                    piece, interp_ref[t], preferred_element_type=jnp.float32
                )
            total = jnp.where(table == t, value, total)
        added = jnp.zeros((blocks, BW), jnp.float32)
        for piece in thirds(total)[1::-1]:
            added = added + jnp.dot(hot, piece, preferred_element_type=jnp.float32)
        out_ref[:, cols] = volume_ref[:, cols].astype(jnp.float32) + added


def weigh(step, width, images_ref, hot_ref, ctf_ref, out_ref):
    hot = hot_ref[...].astype(jnp.bfloat16)
    half = width // 2
    values = jnp.zeros((images_ref.shape[0], half), jnp.float32)
    for piece in thirds(ctf_ref[:, pl.ds(pl.multiple_of(step * half, half), half)])[::-1]:
        values = values + jnp.dot(hot, piece, preferred_element_type=jnp.float32)
    for k in range(half // BW):
        factor = values[:, k * BW : (k + 1) * BW]
        for part in range(2):
            start = step * width + (2 * k + part) * BW
            cols = pl.ds(pl.multiple_of(start, BW), BW)
            out_ref[:, cols] = (images_ref[:, cols].astype(jnp.float32) * factor).astype(
                jnp.bfloat16
            )


def main_kernel(
    target_ref,
    gathered_ref,
    weighted_ref,
    hot_ref,
    ctf_ref,
    cos_ref,
    sin_ref,
    out_real,
    out_imag,
    evidence_ref,
    wide,
    real_rows,
    imag_rows,
    powers,
    rotated,
    scores,
    weights,
):
    shifts = cos_ref.shape[1]
    count = weighted_ref.shape[0]
    slots = gathered_ref.shape[0]
    step = 256

    @pl.loop(0, slots // step)
    def _(i):
        rows = pl.ds(pl.multiple_of(i * step, step), step)
        wide[rows, :] = gathered_ref[rows, :].astype(jnp.float32)
        out_real[rows, :] = jnp.zeros((step, BW), jnp.float32)
        out_imag[rows, :] = jnp.zeros((step, BW), jnp.float32)

    scores[...] = jnp.zeros_like(scores)

    @pl.loop(0, KB // GROUP)
    def _(i):
        for k in range(GROUP):
            b = i * GROUP + k
            for r in range(R):
                row = wide[pl.ds(target_ref[r * KB + b], 1), :]
                real_rows[k, r : r + 1, :] = row[:, :BW]
                imag_rows[k, r : r + 1, :] = row[:, BW:]
        for k in range(GROUP):
            b = i * GROUP + k
            real = real_rows[k]
            imag = imag_rows[k]
            powers[:, pl.ds(pl.multiple_of(b * BW, BW), BW)] = real * real + imag * imag
            for s in range(shifts):
                c = cos_ref[b, s : s + 1, :]
                n = sin_ref[b, s : s + 1, :]
                rows = slice(s * R, (s + 1) * R)
                rotated[rows, 2 * k * BW : (2 * k + 1) * BW] = (real * c - imag * n).astype(
                    jnp.bfloat16
                )
                rotated[rows, (2 * k + 1) * BW : (2 * k + 2) * BW] = (
                    real * n + imag * c
                ).astype(jnp.bfloat16)
        width = GROUP * 2 * BW
        part = weighted_ref[:, pl.ds(pl.multiple_of(i * width, width), width)]
        scores[...] += lax.dot_general(
            rotated[...], part, (((1,), (1,)), ((), ())), preferred_element_type=jnp.float32
        )

    ctf = ctf_ref[...]
    norms = lax.dot_general(
        powers[...],
        ctf * ctf,
        (((1,), (1,)), ((), ())),
        precision=exact_mode,
        preferred_element_type=jnp.float32,
    )
    image_norms = lax.dot_general(
        norms,
        hot_ref[...],
        (((1,), (1,)), ((), ())),
        precision=exact_mode,
        preferred_element_type=jnp.float32,
    )
    scale = 1.0 / math.sqrt(KB * BW)
    values = (scores[...].reshape(shifts, R, count) - 0.5 * image_norms[None]) * scale
    most = jnp.max(jnp.max(values, axis=0), axis=0, keepdims=True)
    exponent = jnp.exp(values - most[None])
    summed = jnp.sum(jnp.sum(exponent, axis=0), axis=0, keepdims=True)
    evidence_ref[...] = most + jnp.log(summed)
    weights[...] = (exponent / summed[None]).astype(jnp.bfloat16).reshape(shifts * R, count)

    @pl.loop(0, KB)
    def _(b):
        part = weighted_ref[:, pl.ds(pl.multiple_of(b * 2 * BW, 2 * BW), 2 * BW)]
        real = jnp.zeros((R, BW), jnp.float32)
        imag = jnp.zeros((R, BW), jnp.float32)
        for s in range(shifts):
            product = jnp.dot(
                weights[s * R : (s + 1) * R, :], part, preferred_element_type=jnp.float32
            )
            c = cos_ref[b, s : s + 1, :]
            n = sin_ref[b, s : s + 1, :]
            real = real + product[:, :BW] * c + product[:, BW:] * n
            imag = imag + product[:, BW:] * c - product[:, :BW] * n
        k = lax.rem(b, 2)
        real_rows[k] = real
        imag_rows[k] = imag
        for r in range(R):
            row = pl.ds(target_ref[r * KB + b], 1)
            out_real[row, :] = real_rows[k, r : r + 1, :]
            out_imag[row, :] = imag_rows[k, r : r + 1, :]


def split_axes(devices):
    pairs = devices // 2
    middle = 1
    while 4 * middle * middle <= pairs:
        middle *= 2
    return pairs // middle, middle


def place_of(devices):
    outer, middle = split_axes(devices)
    me = lax.axis_index("img")
    return outer, middle, me // (2 * middle), (me // 2) % middle, me % 2


def greet(outer, middle, a, b, c, device):
    barrier = pltpu.get_barrier_semaphore()
    peers = [device((a + d) % outer, b, c) for d in range(1, outer)]
    peers += [device(a, (b + d) % middle, c) for d in range(1, middle)]
    peers += [device(a, b, 1 - c)]
    for peer in peers:
        pl.semaphore_signal(
            barrier, inc=1, device_id={"img": peer}, device_id_type=pl.DeviceIdType.MESH
        )
    pl.semaphore_wait(barrier, len(peers))


def spread_kernel(
    devices,
    own_ref,
    images_ref,
    hot_ref,
    ctf_ref,
    out_ref,
    weighted_ref,
    sem_a,
    sem_b,
    sem_c,
    sem_own,
):
    outer, middle, a, b, c = place_of(devices)

    def device(a, b, c):
        return (a * middle + b) * 2 + c

    def slot(a, b, c):
        return (c * middle + b) * outer + a

    def send(src, where, sems, peer):
        copy = pltpu.make_async_remote_copy(
            src_ref=src,
            dst_ref=out_ref.at[where],
            send_sem=sems[0],
            recv_sem=sems[1],
            device_id={"img": peer},
            device_id_type=pl.DeviceIdType.MESH,
        )
        copy.start()
        return copy

    greet(outer, middle, a, b, c, device)
    keep = pltpu.make_async_copy(own_ref, out_ref.at[slot(a, b, c)], sem_own)
    keep.start()
    first, second, third = {}, {}, {}

    def to_core(da, db):
        where = slot((a - da + outer) % outer, (b - db + middle) % middle, c)
        src = own_ref if da == 0 and db == 0 else out_ref.at[where]
        sems = (sem_c.at[0, da, db], sem_c.at[1, da, db])
        third[da, db] = send(src, where, sems, device(a, b, 1 - c))

    def to_middle(da):
        where = slot((a - da + outer) % outer, b, c)
        src = own_ref if da == 0 else out_ref.at[where]
        for db in range(1, middle):
            sems = (sem_b.at[0, da, db], sem_b.at[1, da, db])
            second[da, db] = send(src, where, sems, device(a, (b + db) % middle, c))

    here = slot(a, b, c)
    to_middle(0)
    for d in range(1, outer):
        first[d] = send(
            own_ref, here, (sem_a.at[0, d], sem_a.at[1, d]), device((a + d) % outer, b, c)
        )
    to_core(0, 0)
    width = 1024
    steps = images_ref.shape[1] // width

    @pl.loop(0, steps // 2)
    def _(i):
        weigh(i, width, images_ref, hot_ref, ctf_ref, weighted_ref)

    for db in range(1, middle):
        second[0, db].wait_recv()
        to_core(0, db)
    for d in sorted(range(1, outer), key=lambda d: min(d, outer - d)):
        first[d].wait_recv()
        to_middle(d)
        to_core(d, 0)
        if min(d, outer - d) == 1 and d != 1:

            @pl.loop(steps // 2, steps)
            def _(i):
                weigh(i, width, images_ref, hot_ref, ctf_ref, weighted_ref)

    for d in range(1, outer):
        for db in range(1, middle):
            second[d, db].wait_recv()
            to_core(d, db)
    keep.wait()
    for copy in list(first.values()) + list(second.values()):
        copy.wait_send()
    for copy in third.values():
        copy.wait()


def collect_kernel(
    devices,
    real_ref,
    imag_ref,
    out_real,
    out_imag,
    core_box,
    middle_out,
    middle_box,
    outer_out,
    outer_box,
    sem_c,
    sem_b,
    sem_a,
):
    outer, middle, a, b, c = place_of(devices)
    inputs = (real_ref, imag_ref)

    def device(a, b, c):
        return (a * middle + b) * 2 + c

    def send(src, dst, sems, peer):
        copy = pltpu.make_async_remote_copy(
            src_ref=src,
            dst_ref=dst,
            send_sem=sems[0],
            recv_sem=sems[1],
            device_id={"img": peer},
            device_id_type=pl.DeviceIdType.MESH,
        )
        copy.start()
        return copy

    greet(outer, middle, a, b, c, device)
    order = list(range(1, middle)) + [0]
    first, second, third = {}, {}, {}
    for db in order:
        bq = (b + db) % middle
        for part in range(2):
            first[db, part] = send(
                inputs[part].at[1 - c, bq],
                core_box.at[db, part],
                (sem_c.at[0, db, part], sem_c.at[1, db, part]),
                device(a, b, 1 - c),
            )

    def pair_sum(db, da, part):
        bq = (b + db) % middle
        aq = (a + da) % outer
        return inputs[part][c, bq, aq] + core_box[db, part, aq]

    steps = list(range(1, outer)) + [0]
    for db in range(1, middle):
        first[db, 0].wait_recv()
        first[db, 1].wait_recv()
        for da in steps:
            for part in range(2):
                middle_out[db - 1, da, part] = pair_sum(db, da, part).astype(jnp.bfloat16)
            second[db, da] = send(
                middle_out.at[db - 1, da],
                middle_box.at[db - 1, da],
                (sem_b.at[0, db, da], sem_b.at[1, db, da]),
                device(a, (b + db) % middle, c),
            )
    first[0, 0].wait_recv()
    first[0, 1].wait_recv()
    outs = (out_real, out_imag)
    for da in steps:
        for db in range(1, middle):
            second[db, da].wait_recv()
        for part in range(2):
            total = pair_sum(0, da, part)
            for db in range(1, middle):
                total = total + middle_box[db - 1, da, part].astype(jnp.float32)
            if da:
                outer_out[da - 1, part] = total.astype(jnp.bfloat16)
            else:
                outs[part][...] = total
        if da:
            third[da] = send(
                outer_out.at[da - 1],
                outer_box.at[da - 1],
                (sem_a.at[0, da], sem_a.at[1, da]),
                device((a + da) % outer, b, c),
            )
    for da in range(1, outer):
        third[da].wait_recv()
        for part in range(2):
            outs[part][...] += outer_box[da - 1, part].astype(jnp.float32)
    for copy in list(first.values()) + list(second.values()) + list(third.values()):
        copy.wait_send()


def spread(own, images, hot, ctf, devices):
    outer, middle = split_axes(devices)
    return pl.pallas_call(
        functools.partial(spread_kernel, devices),
        out_shape=(
            jax.ShapeDtypeStruct((devices,) + own.shape, own.dtype),
            jax.ShapeDtypeStruct(images.shape, images.dtype),
        ),
        in_specs=[pl.BlockSpec(memory_space=VMEM)] * 4,
        out_specs=(pl.BlockSpec(memory_space=VMEM),) * 2,
        scratch_shapes=[
            pltpu.SemaphoreType.DMA((2, outer)),
            pltpu.SemaphoreType.DMA((2, outer, middle)),
            pltpu.SemaphoreType.DMA((2, outer, middle)),
            pltpu.SemaphoreType.DMA,
        ],
        compiler_params=pltpu.CompilerParams(
            collective_id=0, has_side_effects=True, vmem_limit_bytes=24 << 20
        ),
        name="spread",
    )(own, images, hot, ctf)


def collect(real, imag, devices, capacity):
    outer, middle = split_axes(devices)
    shape = (2, middle, outer, capacity, BW)
    most = max(1, middle - 1)
    return pl.pallas_call(
        functools.partial(collect_kernel, devices),
        out_shape=(jax.ShapeDtypeStruct((capacity, BW), jnp.float32),) * 2,
        in_specs=[pl.BlockSpec(memory_space=VMEM)] * 2,
        out_specs=(pl.BlockSpec(memory_space=VMEM),) * 2,
        scratch_shapes=[
            VMEM((middle, 2, outer, capacity, BW), jnp.float32),
            VMEM((most, outer, 2, capacity, BW), jnp.bfloat16),
            VMEM((most, outer, 2, capacity, BW), jnp.bfloat16),
            VMEM((max(1, outer - 1), 2, capacity, BW), jnp.bfloat16),
            VMEM((max(1, outer - 1), 2, capacity, BW), jnp.bfloat16),
            pltpu.SemaphoreType.DMA((2, middle, 2)),
            pltpu.SemaphoreType.DMA((2, middle, outer)),
            pltpu.SemaphoreType.DMA((2, outer)),
        ],
        compiler_params=pltpu.CompilerParams(
            collective_id=1, has_side_effects=True, vmem_limit_bytes=40 << 20
        ),
        name="collect",
    )(real.reshape(shape), imag.reshape(shape))


def per_device(images, groups, shifts, volume, owner, local, table_id, interp, ctf):
    devices = lax.axis_size("img")
    block_count = R * KB
    count = images.shape[0]
    blocks = volume.shape[0]
    tries = shifts.shape[0]
    capacity = max(2, 3 * block_count // (2 * devices))
    slots = devices * capacity
    owners = owner[:, 0]

    lines = block_count // BW
    spare = jnp.zeros((lines, 5, BW), jnp.int32)
    columns = [x.reshape(lines, 1, BW) for x in (local // 256, local % 256, table_id)]
    own_slices, target, slot_local, slot_table = pl.pallas_call(
        functools.partial(prep_kernel, devices),
        out_shape=(
            jax.ShapeDtypeStruct((capacity, 2 * BW), jnp.bfloat16),
            jax.ShapeDtypeStruct((lines, BW), jnp.int32),
            jax.ShapeDtypeStruct((1, capacity), jnp.int32),
            jax.ShapeDtypeStruct((capacity, 1), jnp.int32),
        ),
        name="prep",
    )(owners.reshape(lines, BW), jnp.concatenate(columns + [spare], axis=1), volume, interp)
    target = target.reshape(block_count)

    hot = (groups[:, None] == jnp.arange(ctf.shape[0])[None, :]).astype(jnp.float32)
    gathered, weighted = spread(own_slices, images, hot, ctf, devices)
    gathered = gathered.reshape(slots, 2 * BW)
    cosine, sine = phases(shifts)

    out_real, out_imag, evidence = pl.pallas_call(
        main_kernel,
        out_shape=(
            jax.ShapeDtypeStruct((slots, BW), jnp.float32),
            jax.ShapeDtypeStruct((slots, BW), jnp.float32),
            jax.ShapeDtypeStruct((1, count), jnp.float32),
        ),
        in_specs=[pl.BlockSpec(memory_space=pltpu.SMEM)]
        + [pl.BlockSpec(memory_space=VMEM)] * 6,
        out_specs=(pl.BlockSpec(memory_space=VMEM),) * 3,
        scratch_shapes=[
            VMEM((slots, 2 * BW), jnp.float32),
            VMEM((GROUP, R, BW), jnp.float32),
            VMEM((GROUP, R, BW), jnp.float32),
            VMEM((R, KB * BW), jnp.float32),
            VMEM((tries * R, GROUP * 2 * BW), jnp.bfloat16),
            VMEM((tries * R, count), jnp.float32),
            VMEM((tries * R, count), jnp.bfloat16),
        ],
        compiler_params=pltpu.CompilerParams(vmem_limit_bytes=48 << 20),
        name="score",
    )(target, gathered, weighted, hot, ctf, cosine, sine)

    received_real, received_imag = collect(out_real, out_imag, devices, capacity)
    new_map = pl.pallas_call(
        end_kernel,
        out_shape=jax.ShapeDtypeStruct((blocks, 2 * BW), jnp.float32),
        name="finish",
    )(slot_local, slot_table, received_real, received_imag, volume, interp)
    return (new_map, evidence.reshape(count))


def solution(mesh):
    return jax.shard_map(
        per_device,
        mesh=mesh,
        in_specs=(
            P(("parts", "img"), None),
            P(("parts", "img")),
            P("parts", None),
            P(("parts", "img"), None),
            P("parts", None),
            P("parts"),
            P("parts"),
            P(),
            P("parts", None),
        ),
        out_specs=(P(("parts", "img"), None), P(("parts", "img"))),
        check_vma=False,
    )
```

```python
import functools
import math

import jax
import jax.numpy as jnp
from jax import lax
from jax.experimental import pallas as pl
from jax.experimental.pallas import tpu as pltpu
from jax.sharding import PartitionSpec as P

BW = 128
KB = 64
R = 64
GROUP = 4

exact_mode = lax.Precision.HIGHEST
VMEM = pltpu.VMEM


def phases(shifts):
    freq_x = (jnp.arange(BW) - BW // 2).astype(jnp.float32)
    freq_y = jnp.arange(KB).astype(jnp.float32)
    shift_x = shifts[:, 0].astype(jnp.float32)
    shift_y = shifts[:, 1].astype(jnp.float32)
    angles = (
        2.0
        * math.pi
        / BW
        * (
            shift_x[None, :, None] * freq_x[None, None, :]
            + shift_y[None, :, None] * freq_y[:, None, None]
        )
    )
    return (jnp.cos(angles), jnp.sin(angles))


def thirds(x):
    high = x.astype(jnp.bfloat16)
    rest = x - high.astype(jnp.float32)
    mid = rest.astype(jnp.bfloat16)
    low = (rest - mid.astype(jnp.float32)).astype(jnp.bfloat16)
    return (high, mid, low)


def prep_kernel(
    devices, owner_ref, local_ref, id_ref, volume_ref, interp_ref, out_ref, target_ref, row_ref, table_ref
):
    lines = owner_ref.shape[0]
    count = out_ref.shape[0]
    blocks = volume_ref.shape[0]
    outer, middle = split_axes(devices)
    me = lax.axis_index("img")
    owner = owner_ref[...]
    bits = jnp.bfloat16

    def one(condition):
        return jnp.where(condition, 1.0, 0.0).astype(bits)

    def index(shape, axis):
        return lax.broadcasted_iota(jnp.int32, shape, axis)

    upto = one(index((BW, BW), 0) <= index((BW, BW), 1))
    earlier = one(index((lines, lines), 1) < index((lines, lines), 0))
    every = jnp.ones((BW, BW), bits)
    target = jnp.zeros((lines, BW), jnp.float32)
    for o in range(devices):
        mine = one(owner == o)
        rank = jnp.dot(mine, upto, preferred_element_type=jnp.float32)
        above = jnp.dot(earlier, mine, preferred_element_type=jnp.float32).astype(bits)
        rank = rank + jnp.dot(above, every, preferred_element_type=jnp.float32)
        order = ((o % 2) * middle + (o // 2) % middle) * outer + o // (2 * middle)
        target = jnp.where(owner == o, rank + (order * count - 1.0), target)
    target = target.astype(jnp.int32)
    target_ref[...] = target

    order = ((me % 2) * middle + (me // 2) % middle) * outer + me // (2 * middle)
    place = target - order * count
    slot_rows = jnp.zeros((8, count), jnp.float32)
    slot_columns = jnp.zeros((count, 8), jnp.float32)
    wanted = index((count, BW), 0)
    locals_ = local_ref[...]
    high = (locals_ >> 8).astype(jnp.float32)
    low = (locals_ & 255).astype(jnp.float32)
    ids = id_ref[...].astype(jnp.float32)
    blank = jnp.zeros((5, BW), jnp.float32)
    for k in range(lines):
        chosen = one(place[k : k + 1, :] == wanted)
        info = jnp.concatenate(
            [high[k : k + 1], low[k : k + 1], ids[k : k + 1], blank], axis=0
        ).astype(bits)
        dims = (((1,), (1,)), ((), ()))
        slot_rows = slot_rows + lax.dot_general(
            info, chosen, dims, preferred_element_type=jnp.float32
        )
        slot_columns = slot_columns + lax.dot_general(
            chosen, info, dims, preferred_element_type=jnp.float32
        )
    slot_rows = slot_rows.astype(jnp.int32)
    slot_columns = slot_columns.astype(jnp.int32)
    row_ref[...] = slot_rows[0:1] * 256 + slot_rows[1:2]
    local = slot_columns[:, 0:1] * 256 + slot_columns[:, 1:2]
    table = slot_columns[:, 2:3]
    table_ref[...] = table

    hot = one(local == index((count, blocks), 1))
    rows = jnp.dot(hot, volume_ref[...], preferred_element_type=jnp.float32).astype(bits)
    for part in range(2):
        piece = rows[:, part * BW : (part + 1) * BW]
        total = jnp.zeros((count, BW), jnp.float32)
        for t in range(interp_ref.shape[0]):
            value = lax.dot_general(
                piece, interp_ref[t], (((1,), (1,)), ((), ())), preferred_element_type=jnp.float32
            )
            total = jnp.where(table == t, value, total)
        out_ref[:, part * BW : (part + 1) * BW] = total.astype(bits)


def end_kernel(local_ref, table_ref, real_ref, imag_ref, volume_ref, interp_ref, out_ref):
    count = table_ref.shape[0]
    blocks = volume_ref.shape[0]
    hot = (
        (local_ref[...] == lax.broadcasted_iota(jnp.int32, (blocks, count), 0))
        .astype(jnp.float32)
        .astype(jnp.bfloat16)
    )
    table = table_ref[...]
    for part, received_ref in enumerate((real_ref, imag_ref)):
        cols = slice(part * BW, (part + 1) * BW)
        total = jnp.zeros((count, BW), jnp.float32)
        pieces = thirds(received_ref[...])[:2]
        for t in range(interp_ref.shape[0]):
            value = jnp.zeros((count, BW), jnp.float32)
            for piece in pieces[::-1]:
                value = value + jnp.dot(
                    piece, interp_ref[t], preferred_element_type=jnp.float32
                )
            total = jnp.where(table == t, value, total)
        added = jnp.zeros((blocks, BW), jnp.float32)
        for piece in thirds(total)[1::-1]:
            added = added + jnp.dot(hot, piece, preferred_element_type=jnp.float32)
        out_ref[:, cols] = volume_ref[:, cols].astype(jnp.float32) + added


def weigh(step, width, images_ref, hot_ref, ctf_ref, out_ref):
    hot = hot_ref[...].astype(jnp.bfloat16)
    half = width // 2
    values = jnp.zeros((images_ref.shape[0], half), jnp.float32)
    for piece in thirds(ctf_ref[:, pl.ds(pl.multiple_of(step * half, half), half)])[::-1]:
        values = values + jnp.dot(hot, piece, preferred_element_type=jnp.float32)
    for k in range(half // BW):
        factor = values[:, k * BW : (k + 1) * BW]
        for part in range(2):
            start = step * width + (2 * k + part) * BW
            cols = pl.ds(pl.multiple_of(start, BW), BW)
            out_ref[:, cols] = (images_ref[:, cols].astype(jnp.float32) * factor).astype(
                jnp.bfloat16
            )


def main_kernel(
    target_ref,
    gathered_ref,
    weighted_ref,
    hot_ref,
    ctf_ref,
    cos_ref,
    sin_ref,
    keep_ref,
    send_ref,
    evidence_ref,
    wide,
    out_real,
    out_imag,
    real_rows,
    imag_rows,
    powers,
    rotated_even,
    rotated_odd,
    scores,
    weights,
    sems,
):
    shifts = cos_ref.shape[1]
    count = weighted_ref.shape[0]
    slots = gathered_ref.shape[0]
    step = 256

    @pl.loop(0, slots // step)
    def _(i):
        rows = pl.ds(pl.multiple_of(i * step, step), step)
        wide[rows, :] = gathered_ref[rows, :].astype(jnp.float32)
        out_real[rows, :] = jnp.zeros((step, BW), jnp.float32)
        out_imag[rows, :] = jnp.zeros((step, BW), jnp.float32)

    scores[...] = jnp.zeros_like(scores)

    def turn(i, rotated, first):
        for k in range(GROUP):
            b = i * GROUP + k
            for r in range(R):
                row = wide[pl.ds(target_ref[r * KB + b], 1), :]
                real_rows[first + k, r : r + 1, :] = row[:, :BW]
                imag_rows[first + k, r : r + 1, :] = row[:, BW:]
        for k in range(GROUP):
            b = i * GROUP + k
            real = real_rows[first + k]
            imag = imag_rows[first + k]
            powers[:, pl.ds(pl.multiple_of(b * BW, BW), BW)] = real * real + imag * imag
            for s in range(shifts):
                c = cos_ref[b, s : s + 1, :]
                n = sin_ref[b, s : s + 1, :]
                rows = slice(s * R, (s + 1) * R)
                rotated[rows, 2 * k * BW : (2 * k + 1) * BW] = (real * c - imag * n).astype(
                    jnp.bfloat16
                )
                rotated[rows, (2 * k + 1) * BW : (2 * k + 2) * BW] = (
                    real * n + imag * c
                ).astype(jnp.bfloat16)
        width = GROUP * 2 * BW
        part = weighted_ref[:, pl.ds(pl.multiple_of(i * width, width), width)]
        return lax.dot_general(
            rotated[...], part, (((1,), (1,)), ((), ())), preferred_element_type=jnp.float32
        )

    @pl.loop(0, KB // GROUP // 2)
    def _(i):
        even = turn(2 * i, rotated_even, 0)
        odd = turn(2 * i + 1, rotated_odd, GROUP)
        scores[...] += even + odd

    ctf = ctf_ref[...]
    norms = lax.dot_general(
        powers[...],
        ctf * ctf,
        (((1,), (1,)), ((), ())),
        precision=exact_mode,
        preferred_element_type=jnp.float32,
    )
    image_norms = lax.dot_general(
        norms,
        hot_ref[...],
        (((1,), (1,)), ((), ())),
        precision=exact_mode,
        preferred_element_type=jnp.float32,
    )
    scale = 1.0 / math.sqrt(KB * BW)
    values = (scores[...].reshape(shifts, R, count) - 0.5 * image_norms[None]) * scale
    most = jnp.max(jnp.max(values, axis=0), axis=0, keepdims=True)
    exponent = jnp.exp(values - most[None])
    summed = jnp.sum(jnp.sum(exponent, axis=0), axis=0, keepdims=True)
    evidence_ref[...] = most + jnp.log(summed)
    weights[...] = (exponent / summed[None]).astype(jnp.bfloat16).reshape(shifts * R, count)

    def back(b, k):
        part = weighted_ref[:, pl.ds(pl.multiple_of(b * 2 * BW, 2 * BW), 2 * BW)]
        real = jnp.zeros((R, BW), jnp.float32)
        imag = jnp.zeros((R, BW), jnp.float32)
        for s in range(shifts):
            product = jnp.dot(
                weights[s * R : (s + 1) * R, :], part, preferred_element_type=jnp.float32
            )
            c = cos_ref[b, s : s + 1, :]
            n = sin_ref[b, s : s + 1, :]
            real = real + product[:, :BW] * c + product[:, BW:] * n
            imag = imag + product[:, BW:] * c - product[:, :BW] * n
        real_rows[k] = real
        imag_rows[k] = imag

    def place(b, k):
        for r in range(R):
            row = pl.ds(target_ref[r * KB + b], 1)
            out_real[row, :] = real_rows[k, r : r + 1, :]
            out_imag[row, :] = imag_rows[k, r : r + 1, :]

    @pl.loop(0, KB // GROUP)
    def _(i):
        for k in range(GROUP):
            back(i * GROUP + k, k)
            if k:
                place(i * GROUP + k - 1, k - 1)
        place(i * GROUP + GROUP - 1, GROUP - 1)

    half = slots // 2
    core = lax.axis_index("img") % 2
    mine = pl.multiple_of(core * half, half)
    other = pl.multiple_of((1 - core) * half, half)
    copies = []
    for part, out in enumerate((out_real, out_imag)):
        copy = pltpu.make_async_copy(out.at[pl.ds(mine, half)], keep_ref.at[part], sems.at[part])
        copy.start()
        copies.append(copy)

    @pl.loop(0, half // step)
    def _(i):
        start = pl.multiple_of(i * step, step)
        for part, out in enumerate((out_real, out_imag)):
            send_ref[part, pl.ds(start, step), :] = out[
                pl.ds(pl.multiple_of(other + start, step), step), :
            ].astype(jnp.bfloat16)

    for copy in copies:
        copy.wait()


def split_axes(devices):
    pairs = devices // 2
    middle = 1
    while 4 * middle * middle <= pairs:
        middle *= 2
    return pairs // middle, middle


def place_of(devices):
    outer, middle = split_axes(devices)
    me = lax.axis_index("img")
    return outer, middle, me // (2 * middle), (me // 2) % middle, me % 2


def greet(outer, middle, a, b, c, device):
    barrier = pltpu.get_barrier_semaphore()
    peers = [device((a + d) % outer, b, c) for d in range(1, outer)]
    peers += [device(a, (b + d) % middle, c) for d in range(1, middle)]
    peers += [device(a, b, 1 - c)]
    for peer in peers:
        pl.semaphore_signal(
            barrier, inc=1, device_id={"img": peer}, device_id_type=pl.DeviceIdType.MESH
        )
    pl.semaphore_wait(barrier, len(peers))


def spread_kernel(
    devices,
    own_ref,
    images_ref,
    hot_ref,
    ctf_ref,
    out_ref,
    weighted_ref,
    sem_a,
    sem_b,
    sem_c,
    sem_own,
):
    outer, middle, a, b, c = place_of(devices)

    def device(a, b, c):
        return (a * middle + b) * 2 + c

    def slot(a, b, c):
        return (c * middle + b) * outer + a

    def send(src, where, sems, peer):
        copy = pltpu.make_async_remote_copy(
            src_ref=src,
            dst_ref=out_ref.at[where],
            send_sem=sems[0],
            recv_sem=sems[1],
            device_id={"img": peer},
            device_id_type=pl.DeviceIdType.MESH,
        )
        copy.start()
        return copy

    greet(outer, middle, a, b, c, device)
    keep = pltpu.make_async_copy(own_ref, out_ref.at[slot(a, b, c)], sem_own)
    keep.start()
    first, second, third = {}, {}, {}

    def to_core(da, db):
        where = slot((a - da + outer) % outer, (b - db + middle) % middle, c)
        src = own_ref if da == 0 and db == 0 else out_ref.at[where]
        sems = (sem_c.at[0, da, db], sem_c.at[1, da, db])
        third[da, db] = send(src, where, sems, device(a, b, 1 - c))

    def to_middle(da):
        where = slot((a - da + outer) % outer, b, c)
        src = own_ref if da == 0 else out_ref.at[where]
        for db in range(1, middle):
            sems = (sem_b.at[0, da, db], sem_b.at[1, da, db])
            second[da, db] = send(src, where, sems, device(a, (b + db) % middle, c))

    here = slot(a, b, c)
    to_middle(0)
    for d in range(1, outer):
        first[d] = send(
            own_ref, here, (sem_a.at[0, d], sem_a.at[1, d]), device((a + d) % outer, b, c)
        )
    to_core(0, 0)
    width = 1024
    steps = images_ref.shape[1] // width

    @pl.loop(0, steps // 2)
    def _(i):
        weigh(i, width, images_ref, hot_ref, ctf_ref, weighted_ref)

    for db in range(1, middle):
        second[0, db].wait_recv()
        to_core(0, db)
    for d in sorted(range(1, outer), key=lambda d: min(d, outer - d)):
        first[d].wait_recv()
        to_middle(d)
        to_core(d, 0)
        if min(d, outer - d) == 1 and d != 1:

            @pl.loop(steps // 2, steps)
            def _(i):
                weigh(i, width, images_ref, hot_ref, ctf_ref, weighted_ref)

    for d in range(1, outer):
        for db in range(1, middle):
            second[d, db].wait_recv()
            to_core(d, db)
    keep.wait()
    for copy in list(first.values()) + list(second.values()):
        copy.wait_send()
    for copy in third.values():
        copy.wait()


def collect_kernel(
    devices,
    keep_ref,
    leave_ref,
    out_real,
    out_imag,
    own_box,
    core_box,
    middle_out,
    middle_box,
    outer_out,
    outer_box,
    sem_own,
    sem_c,
    sem_b,
    sem_a,
):
    outer, middle, a, b, c = place_of(devices)

    def device(a, b, c):
        return (a * middle + b) * 2 + c

    def send(src, dst, sems, peer):
        copy = pltpu.make_async_remote_copy(
            src_ref=src,
            dst_ref=dst,
            send_sem=sems[0],
            recv_sem=sems[1],
            device_id={"img": peer},
            device_id_type=pl.DeviceIdType.MESH,
        )
        copy.start()
        return copy

    order = list(range(1, middle)) + [0]
    own = {}
    for db in order:
        for part in range(2):
            own[db, part] = pltpu.make_async_copy(
                keep_ref.at[part, (b + db) % middle], own_box.at[db, part], sem_own.at[db, part]
            )
            own[db, part].start()
    greet(outer, middle, a, b, c, device)
    first, second, third = {}, {}, {}
    for db in order:
        bq = (b + db) % middle
        for part in range(2):
            first[db, part] = send(
                leave_ref.at[part, bq],
                core_box.at[db, part],
                (sem_c.at[0, db, part], sem_c.at[1, db, part]),
                device(a, b, 1 - c),
            )

    def pair_sum(db, da, part):
        aq = (a + da) % outer
        return own_box[db, part, aq] + core_box[db, part, aq].astype(jnp.float32)

    steps = list(range(1, outer)) + [0]
    for db in range(1, middle):
        for part in range(2):
            own[db, part].wait()
            first[db, part].wait_recv()
        for da in steps:
            for part in range(2):
                middle_out[db - 1, da, part] = pair_sum(db, da, part).astype(jnp.bfloat16)
            second[db, da] = send(
                middle_out.at[db - 1, da],
                middle_box.at[db - 1, da],
                (sem_b.at[0, db, da], sem_b.at[1, db, da]),
                device(a, (b + db) % middle, c),
            )
    for part in range(2):
        own[0, part].wait()
        first[0, part].wait_recv()
    outs = (out_real, out_imag)
    for da in steps:
        for db in range(1, middle):
            second[db, da].wait_recv()
        for part in range(2):
            total = pair_sum(0, da, part)
            for db in range(1, middle):
                total = total + middle_box[db - 1, da, part].astype(jnp.float32)
            if da:
                outer_out[da - 1, part] = total.astype(jnp.bfloat16)
            else:
                outs[part][...] = total
        if da:
            third[da] = send(
                outer_out.at[da - 1],
                outer_box.at[da - 1],
                (sem_a.at[0, da], sem_a.at[1, da]),
                device((a + da) % outer, b, c),
            )
    for da in range(1, outer):
        third[da].wait_recv()
        for part in range(2):
            outs[part][...] += outer_box[da - 1, part].astype(jnp.float32)
    for copy in list(first.values()) + list(second.values()) + list(third.values()):
        copy.wait_send()


def spread(own, images, hot, ctf, devices):
    outer, middle = split_axes(devices)
    return pl.pallas_call(
        functools.partial(spread_kernel, devices),
        out_shape=(
            jax.ShapeDtypeStruct((devices,) + own.shape, own.dtype),
            jax.ShapeDtypeStruct(images.shape, images.dtype),
        ),
        in_specs=[pl.BlockSpec(memory_space=VMEM)] * 4,
        out_specs=(pl.BlockSpec(memory_space=VMEM),) * 2,
        scratch_shapes=[
            pltpu.SemaphoreType.DMA((2, outer)),
            pltpu.SemaphoreType.DMA((2, outer, middle)),
            pltpu.SemaphoreType.DMA((2, outer, middle)),
            pltpu.SemaphoreType.DMA,
        ],
        compiler_params=pltpu.CompilerParams(
            collective_id=0, has_side_effects=True, vmem_limit_bytes=24 << 20
        ),
        name="spread",
    )(own, images, hot, ctf)


def collect(keep, leave, devices, capacity):
    outer, middle = split_axes(devices)
    shape = (2, middle, outer, capacity, BW)
    box = (middle, 2, outer, capacity, BW)
    most = max(1, middle - 1)
    return pl.pallas_call(
        functools.partial(collect_kernel, devices),
        out_shape=(jax.ShapeDtypeStruct((capacity, BW), jnp.float32),) * 2,
        in_specs=[pl.BlockSpec(memory_space=pl.ANY)] * 2,
        out_specs=(pl.BlockSpec(memory_space=VMEM),) * 2,
        scratch_shapes=[
            VMEM(box, jnp.float32),
            VMEM(box, jnp.bfloat16),
            VMEM((most, outer, 2, capacity, BW), jnp.bfloat16),
            VMEM((most, outer, 2, capacity, BW), jnp.bfloat16),
            VMEM((max(1, outer - 1), 2, capacity, BW), jnp.bfloat16),
            VMEM((max(1, outer - 1), 2, capacity, BW), jnp.bfloat16),
            pltpu.SemaphoreType.DMA((middle, 2)),
            pltpu.SemaphoreType.DMA((2, middle, 2)),
            pltpu.SemaphoreType.DMA((2, middle, outer)),
            pltpu.SemaphoreType.DMA((2, outer)),
        ],
        compiler_params=pltpu.CompilerParams(
            collective_id=1, has_side_effects=True, vmem_limit_bytes=40 << 20
        ),
        name="collect",
    )(keep.reshape(shape), leave.reshape(shape))


def per_device(images, groups, shifts, volume, owner, local, table_id, interp, ctf):
    devices = lax.axis_size("img")
    block_count = R * KB
    count = images.shape[0]
    blocks = volume.shape[0]
    tries = shifts.shape[0]
    capacity = max(2, 3 * block_count // (2 * devices))
    slots = devices * capacity
    owners = owner[:, 0]

    lines = block_count // BW
    own_slices, target, slot_local, slot_table = pl.pallas_call(
        functools.partial(prep_kernel, devices),
        out_shape=(
            jax.ShapeDtypeStruct((capacity, 2 * BW), jnp.bfloat16),
            jax.ShapeDtypeStruct((lines, BW), jnp.int32),
            jax.ShapeDtypeStruct((1, capacity), jnp.int32),
            jax.ShapeDtypeStruct((capacity, 1), jnp.int32),
        ),
        name="prep",
    )(
        owners.reshape(lines, BW),
        local.reshape(lines, BW),
        table_id.reshape(lines, BW),
        volume,
        interp,
    )
    target = target.reshape(block_count)

    hot = (groups[:, None] == jnp.arange(ctf.shape[0])[None, :]).astype(jnp.float32)
    gathered, weighted = spread(own_slices, images, hot, ctf, devices)
    gathered = gathered.reshape(slots, 2 * BW)
    cosine, sine = phases(shifts)

    keep, leave, evidence = pl.pallas_call(
        main_kernel,
        out_shape=(
            jax.ShapeDtypeStruct((2, slots // 2, BW), jnp.float32),
            jax.ShapeDtypeStruct((2, slots // 2, BW), jnp.bfloat16),
            jax.ShapeDtypeStruct((1, count), jnp.float32),
        ),
        in_specs=[pl.BlockSpec(memory_space=pltpu.SMEM)]
        + [pl.BlockSpec(memory_space=VMEM)] * 6,
        out_specs=(
            pl.BlockSpec(memory_space=pl.ANY),
            pl.BlockSpec(memory_space=VMEM),
            pl.BlockSpec(memory_space=VMEM),
        ),
        scratch_shapes=[
            VMEM((slots, 2 * BW), jnp.float32),
            VMEM((slots, BW), jnp.float32),
            VMEM((slots, BW), jnp.float32),
            VMEM((2 * GROUP, R, BW), jnp.float32),
            VMEM((2 * GROUP, R, BW), jnp.float32),
            VMEM((R, KB * BW), jnp.float32),
            VMEM((tries * R, GROUP * 2 * BW), jnp.bfloat16),
            VMEM((tries * R, GROUP * 2 * BW), jnp.bfloat16),
            VMEM((tries * R, count), jnp.float32),
            VMEM((tries * R, count), jnp.bfloat16),
            pltpu.SemaphoreType.DMA((2,)),
        ],
        compiler_params=pltpu.CompilerParams(vmem_limit_bytes=48 << 20),
        name="score",
    )(target, gathered, weighted, hot, ctf, cosine, sine)

    received_real, received_imag = collect(keep, leave, devices, capacity)
    new_map = pl.pallas_call(
        end_kernel,
        out_shape=jax.ShapeDtypeStruct((blocks, 2 * BW), jnp.float32),
        name="finish",
    )(slot_local, slot_table, received_real, received_imag, volume, interp)
    return (new_map, evidence.reshape(count))


def solution(mesh):
    return jax.shard_map(
        per_device,
        mesh=mesh,
        in_specs=(
            P(("parts", "img"), None),
            P(("parts", "img")),
            P("parts", None),
            P(("parts", "img"), None),
            P("parts", None),
            P("parts"),
            P("parts"),
            P(),
            P("parts", None),
        ),
        out_specs=(P(("parts", "img"), None), P(("parts", "img"))),
        check_vma=False,
    )
```

```python
import functools
import math

import jax
import jax.numpy as jnp
from jax import lax
from jax.experimental import pallas as pl
from jax.experimental.pallas import tpu as pltpu
from jax.sharding import PartitionSpec as P

BW = 128
KB = 64
R = 64
GROUP = 4

exact_mode = lax.Precision.HIGHEST
VMEM = pltpu.VMEM


def phases(shifts):
    freq_x = (jnp.arange(BW) - BW // 2).astype(jnp.float32)
    freq_y = jnp.arange(KB).astype(jnp.float32)
    shift_x = shifts[:, 0].astype(jnp.float32)
    shift_y = shifts[:, 1].astype(jnp.float32)
    angles = (
        2.0
        * math.pi
        / BW
        * (
            shift_x[None, :, None] * freq_x[None, None, :]
            + shift_y[None, :, None] * freq_y[:, None, None]
        )
    )
    return (jnp.cos(angles), jnp.sin(angles))


def thirds(x):
    high = x.astype(jnp.bfloat16)
    rest = x - high.astype(jnp.float32)
    mid = rest.astype(jnp.bfloat16)
    low = (rest - mid.astype(jnp.float32)).astype(jnp.bfloat16)
    return (high, mid, low)


def prep_kernel(
    devices, owner_ref, local_ref, id_ref, volume_ref, interp_ref, out_ref, target_ref, row_ref, table_ref
):
    lines = owner_ref.shape[0]
    count = out_ref.shape[0]
    blocks = volume_ref.shape[0]
    outer, middle = split_axes(devices)
    me = lax.axis_index("img")
    owner = owner_ref[...]
    bits = jnp.bfloat16

    def one(condition):
        return jnp.where(condition, 1.0, 0.0).astype(bits)

    def index(shape, axis):
        return lax.broadcasted_iota(jnp.int32, shape, axis)

    upto = one(index((BW, BW), 0) <= index((BW, BW), 1))
    earlier = one(index((lines, lines), 1) < index((lines, lines), 0))
    every = jnp.ones((BW, BW), bits)
    target = jnp.zeros((lines, BW), jnp.float32)
    for o in range(devices):
        mine = one(owner == o)
        rank = jnp.dot(mine, upto, preferred_element_type=jnp.float32)
        above = jnp.dot(earlier, mine, preferred_element_type=jnp.float32).astype(bits)
        rank = rank + jnp.dot(above, every, preferred_element_type=jnp.float32)
        order = ((o % 2) * middle + (o // 2) % middle) * outer + o // (2 * middle)
        target = jnp.where(owner == o, rank + (order * count - 1.0), target)
    target = target.astype(jnp.int32)
    target_ref[...] = target

    order = ((me % 2) * middle + (me // 2) % middle) * outer + me // (2 * middle)
    place = target - order * count
    slot_rows = jnp.zeros((8, count), jnp.float32)
    slot_columns = jnp.zeros((count, 8), jnp.float32)
    wanted = index((count, BW), 0)
    locals_ = local_ref[...]
    high = (locals_ >> 8).astype(jnp.float32)
    low = (locals_ & 255).astype(jnp.float32)
    ids = id_ref[...].astype(jnp.float32)
    blank = jnp.zeros((5, BW), jnp.float32)
    for k in range(lines):
        chosen = one(place[k : k + 1, :] == wanted)
        info = jnp.concatenate(
            [high[k : k + 1], low[k : k + 1], ids[k : k + 1], blank], axis=0
        ).astype(bits)
        dims = (((1,), (1,)), ((), ()))
        slot_rows = slot_rows + lax.dot_general(
            info, chosen, dims, preferred_element_type=jnp.float32
        )
        slot_columns = slot_columns + lax.dot_general(
            chosen, info, dims, preferred_element_type=jnp.float32
        )
    slot_rows = slot_rows.astype(jnp.int32)
    slot_columns = slot_columns.astype(jnp.int32)
    row_ref[...] = slot_rows[0:1] * 256 + slot_rows[1:2]
    local = slot_columns[:, 0:1] * 256 + slot_columns[:, 1:2]
    table = slot_columns[:, 2:3]
    table_ref[...] = table

    hot = one(local == index((count, blocks), 1))
    rows = jnp.dot(hot, volume_ref[...], preferred_element_type=jnp.float32).astype(bits)
    for part in range(2):
        piece = rows[:, part * BW : (part + 1) * BW]
        total = jnp.zeros((count, BW), jnp.float32)
        for t in range(interp_ref.shape[0]):
            value = lax.dot_general(
                piece, interp_ref[t], (((1,), (1,)), ((), ())), preferred_element_type=jnp.float32
            )
            total = jnp.where(table == t, value, total)
        out_ref[:, part * BW : (part + 1) * BW] = total.astype(bits)


def end_kernel(local_ref, table_ref, real_ref, imag_ref, volume_ref, interp_ref, out_ref):
    count = table_ref.shape[0]
    blocks = volume_ref.shape[0]
    hot = (
        (local_ref[...] == lax.broadcasted_iota(jnp.int32, (blocks, count), 0))
        .astype(jnp.float32)
        .astype(jnp.bfloat16)
    )
    table = table_ref[...]
    for part, received_ref in enumerate((real_ref, imag_ref)):
        cols = slice(part * BW, (part + 1) * BW)
        total = jnp.zeros((count, BW), jnp.float32)
        pieces = thirds(received_ref[...])[:2]
        for t in range(interp_ref.shape[0]):
            value = jnp.zeros((count, BW), jnp.float32)
            for piece in pieces[::-1]:
                value = value + jnp.dot(
                    piece, interp_ref[t], preferred_element_type=jnp.float32
                )
            total = jnp.where(table == t, value, total)
        added = jnp.zeros((blocks, BW), jnp.float32)
        for piece in thirds(total)[1::-1]:
            added = added + jnp.dot(hot, piece, preferred_element_type=jnp.float32)
        out_ref[:, cols] = volume_ref[:, cols].astype(jnp.float32) + added


def weigh(step, width, images_ref, hot_ref, ctf_ref, out_ref):
    hot = hot_ref[...].astype(jnp.bfloat16)
    half = width // 2
    values = jnp.zeros((images_ref.shape[0], half), jnp.float32)
    for piece in thirds(ctf_ref[:, pl.ds(pl.multiple_of(step * half, half), half)])[::-1]:
        values = values + jnp.dot(hot, piece, preferred_element_type=jnp.float32)
    for k in range(half // BW):
        factor = values[:, k * BW : (k + 1) * BW]
        for part in range(2):
            start = step * width + (2 * k + part) * BW
            cols = pl.ds(pl.multiple_of(start, BW), BW)
            out_ref[:, cols] = (images_ref[:, cols].astype(jnp.float32) * factor).astype(
                jnp.bfloat16
            )


def main_kernel(
    target_ref,
    gathered_ref,
    weighted_ref,
    hot_ref,
    ctf_ref,
    cos_ref,
    sin_ref,
    keep_ref,
    send_ref,
    evidence_ref,
    wide,
    out_real,
    out_imag,
    real_rows,
    imag_rows,
    powers,
    rotated_even,
    rotated_odd,
    scores,
    weights,
    sems,
):
    shifts = cos_ref.shape[1]
    count = weighted_ref.shape[0]
    slots = gathered_ref.shape[0]
    step = 256

    @pl.loop(0, slots // step)
    def _(i):
        rows = pl.ds(pl.multiple_of(i * step, step), step)
        wide[rows, :] = gathered_ref[rows, :].astype(jnp.float32)
        out_real[rows, :] = jnp.zeros((step, BW), jnp.float32)
        out_imag[rows, :] = jnp.zeros((step, BW), jnp.float32)

    scores[...] = jnp.zeros_like(scores)

    def turn(i, rotated, first):
        for k in range(GROUP):
            b = i * GROUP + k
            for r in range(R):
                row = wide[pl.ds(target_ref[r * KB + b], 1), :]
                real_rows[first + k, r : r + 1, :] = row[:, :BW]
                imag_rows[first + k, r : r + 1, :] = row[:, BW:]
        for k in range(GROUP):
            b = i * GROUP + k
            real = real_rows[first + k]
            imag = imag_rows[first + k]
            powers[:, pl.ds(pl.multiple_of(b * BW, BW), BW)] = real * real + imag * imag
            for s in range(shifts):
                c = cos_ref[b, s : s + 1, :]
                n = sin_ref[b, s : s + 1, :]
                rows = slice(s * R, (s + 1) * R)
                rotated[rows, 2 * k * BW : (2 * k + 1) * BW] = (real * c - imag * n).astype(
                    jnp.bfloat16
                )
                rotated[rows, (2 * k + 1) * BW : (2 * k + 2) * BW] = (
                    real * n + imag * c
                ).astype(jnp.bfloat16)
        width = GROUP * 2 * BW
        part = weighted_ref[:, pl.ds(pl.multiple_of(i * width, width), width)]
        return lax.dot_general(
            rotated[...], part, (((1,), (1,)), ((), ())), preferred_element_type=jnp.float32
        )

    @pl.loop(0, KB // GROUP // 2)
    def _(i):
        even = turn(2 * i, rotated_even, 0)
        odd = turn(2 * i + 1, rotated_odd, GROUP)
        scores[...] += even + odd

    ctf = ctf_ref[...]
    norms = lax.dot_general(
        powers[...],
        ctf * ctf,
        (((1,), (1,)), ((), ())),
        precision=exact_mode,
        preferred_element_type=jnp.float32,
    )
    image_norms = lax.dot_general(
        norms,
        hot_ref[...],
        (((1,), (1,)), ((), ())),
        precision=exact_mode,
        preferred_element_type=jnp.float32,
    )
    scale = 1.0 / math.sqrt(KB * BW)
    values = (scores[...].reshape(shifts, R, count) - 0.5 * image_norms[None]) * scale
    most = jnp.max(jnp.max(values, axis=0), axis=0, keepdims=True)
    exponent = jnp.exp(values - most[None])
    summed = jnp.sum(jnp.sum(exponent, axis=0), axis=0, keepdims=True)
    evidence_ref[...] = most + jnp.log(summed)
    weights[...] = (exponent / summed[None]).astype(jnp.bfloat16).reshape(shifts * R, count)

    def back(b, k):
        part = weighted_ref[:, pl.ds(pl.multiple_of(b * 2 * BW, 2 * BW), 2 * BW)]
        real = jnp.zeros((R, BW), jnp.float32)
        imag = jnp.zeros((R, BW), jnp.float32)
        for s in range(shifts):
            product = jnp.dot(
                weights[s * R : (s + 1) * R, :], part, preferred_element_type=jnp.float32
            )
            c = cos_ref[b, s : s + 1, :]
            n = sin_ref[b, s : s + 1, :]
            real = real + product[:, :BW] * c + product[:, BW:] * n
            imag = imag + product[:, BW:] * c - product[:, :BW] * n
        real_rows[k] = real
        imag_rows[k] = imag

    def place(b, k):
        for r in range(R):
            row = pl.ds(target_ref[r * KB + b], 1)
            out_real[row, :] = real_rows[k, r : r + 1, :]
            out_imag[row, :] = imag_rows[k, r : r + 1, :]

    trip = 2 * GROUP

    @pl.loop(0, KB // trip)
    def _(i):
        for k in range(trip):
            back(i * trip + k, k)
            if k:
                place(i * trip + k - 1, k - 1)
        place(i * trip + trip - 1, trip - 1)

    half = slots // 2
    core = lax.axis_index("img") % 2
    mine = pl.multiple_of(core * half, half)
    other = pl.multiple_of((1 - core) * half, half)
    copies = []
    for part, out in enumerate((out_real, out_imag)):
        copy = pltpu.make_async_copy(out.at[pl.ds(mine, half)], keep_ref.at[part], sems.at[part])
        copy.start()
        copies.append(copy)

    @pl.loop(0, half // step)
    def _(i):
        start = pl.multiple_of(i * step, step)
        for part, out in enumerate((out_real, out_imag)):
            send_ref[part, pl.ds(start, step), :] = out[
                pl.ds(pl.multiple_of(other + start, step), step), :
            ].astype(jnp.bfloat16)

    for copy in copies:
        copy.wait()


def split_axes(devices):
    pairs = devices // 2
    middle = 1
    while 4 * middle * middle <= pairs:
        middle *= 2
    return pairs // middle, middle


def place_of(devices):
    outer, middle = split_axes(devices)
    me = lax.axis_index("img")
    return outer, middle, me // (2 * middle), (me // 2) % middle, me % 2


def greet(outer, middle, a, b, c, device):
    barrier = pltpu.get_barrier_semaphore()
    peers = [device((a + d) % outer, b, c) for d in range(1, outer)]
    peers += [device(a, (b + d) % middle, c) for d in range(1, middle)]
    peers += [device(a, b, 1 - c)]
    for peer in peers:
        pl.semaphore_signal(
            barrier, inc=1, device_id={"img": peer}, device_id_type=pl.DeviceIdType.MESH
        )
    pl.semaphore_wait(barrier, len(peers))


def spread_kernel(
    devices,
    own_ref,
    images_ref,
    hot_ref,
    ctf_ref,
    out_ref,
    weighted_ref,
    sem_a,
    sem_b,
    sem_c,
    sem_own,
):
    outer, middle, a, b, c = place_of(devices)

    def device(a, b, c):
        return (a * middle + b) * 2 + c

    def slot(a, b, c):
        return (c * middle + b) * outer + a

    def send(src, where, sems, peer):
        copy = pltpu.make_async_remote_copy(
            src_ref=src,
            dst_ref=out_ref.at[where],
            send_sem=sems[0],
            recv_sem=sems[1],
            device_id={"img": peer},
            device_id_type=pl.DeviceIdType.MESH,
        )
        copy.start()
        return copy

    greet(outer, middle, a, b, c, device)
    keep = pltpu.make_async_copy(own_ref, out_ref.at[slot(a, b, c)], sem_own)
    keep.start()
    first, second, third = {}, {}, {}

    def to_core(da, db):
        where = slot((a - da + outer) % outer, (b - db + middle) % middle, c)
        src = own_ref if da == 0 and db == 0 else out_ref.at[where]
        sems = (sem_c.at[0, da, db], sem_c.at[1, da, db])
        third[da, db] = send(src, where, sems, device(a, b, 1 - c))

    def to_middle(da):
        where = slot((a - da + outer) % outer, b, c)
        src = own_ref if da == 0 else out_ref.at[where]
        for db in range(1, middle):
            sems = (sem_b.at[0, da, db], sem_b.at[1, da, db])
            second[da, db] = send(src, where, sems, device(a, (b + db) % middle, c))

    here = slot(a, b, c)
    to_middle(0)
    for d in range(1, outer):
        first[d] = send(
            own_ref, here, (sem_a.at[0, d], sem_a.at[1, d]), device((a + d) % outer, b, c)
        )
    to_core(0, 0)
    width = 1024
    steps = images_ref.shape[1] // width

    @pl.loop(0, steps // 2)
    def _(i):
        weigh(i, width, images_ref, hot_ref, ctf_ref, weighted_ref)

    for db in range(1, middle):
        second[0, db].wait_recv()
        to_core(0, db)
    for d in sorted(range(1, outer), key=lambda d: min(d, outer - d)):
        first[d].wait_recv()
        to_middle(d)
        to_core(d, 0)
        if min(d, outer - d) == 1 and d != 1:

            @pl.loop(steps // 2, steps)
            def _(i):
                weigh(i, width, images_ref, hot_ref, ctf_ref, weighted_ref)

    for d in range(1, outer):
        for db in range(1, middle):
            second[d, db].wait_recv()
            to_core(d, db)
    keep.wait()
    for copy in list(first.values()) + list(second.values()):
        copy.wait_send()
    for copy in third.values():
        copy.wait()


def collect_kernel(
    devices,
    keep_ref,
    leave_ref,
    out_real,
    out_imag,
    own_box,
    core_box,
    middle_out,
    middle_box,
    outer_out,
    outer_box,
    sem_own,
    sem_c,
    sem_b,
    sem_a,
):
    outer, middle, a, b, c = place_of(devices)

    def device(a, b, c):
        return (a * middle + b) * 2 + c

    def send(src, dst, sems, peer):
        copy = pltpu.make_async_remote_copy(
            src_ref=src,
            dst_ref=dst,
            send_sem=sems[0],
            recv_sem=sems[1],
            device_id={"img": peer},
            device_id_type=pl.DeviceIdType.MESH,
        )
        copy.start()
        return copy

    order = list(range(1, middle)) + [0]
    own = {}
    for db in order:
        for part in range(2):
            own[db, part] = pltpu.make_async_copy(
                keep_ref.at[part, (b + db) % middle], own_box.at[db, part], sem_own.at[db, part]
            )
            own[db, part].start()
    greet(outer, middle, a, b, c, device)
    first, second, third = {}, {}, {}
    for db in order:
        bq = (b + db) % middle
        for part in range(2):
            first[db, part] = send(
                leave_ref.at[part, bq],
                core_box.at[db, part],
                (sem_c.at[0, db, part], sem_c.at[1, db, part]),
                device(a, b, 1 - c),
            )

    def pair_sum(db, da, part):
        aq = (a + da) % outer
        return own_box[db, part, aq] + core_box[db, part, aq].astype(jnp.float32)

    steps = sorted(range(1, outer), key=lambda d: -min(d, outer - d)) + [0]
    for db in range(1, middle):
        for part in range(2):
            own[db, part].wait()
            first[db, part].wait_recv()
        for da in steps:
            for part in range(2):
                middle_out[db - 1, da, part] = pair_sum(db, da, part).astype(jnp.bfloat16)
            second[db, da] = send(
                middle_out.at[db - 1, da],
                middle_box.at[db - 1, da],
                (sem_b.at[0, db, da], sem_b.at[1, db, da]),
                device(a, (b + db) % middle, c),
            )
    for part in range(2):
        own[0, part].wait()
        first[0, part].wait_recv()
    outs = (out_real, out_imag)
    for da in steps:
        for db in range(1, middle):
            second[db, da].wait_recv()
        for part in range(2):
            total = pair_sum(0, da, part)
            for db in range(1, middle):
                total = total + middle_box[db - 1, da, part].astype(jnp.float32)
            if da:
                outer_out[da - 1, part] = total.astype(jnp.bfloat16)
            else:
                outs[part][...] = total
        if da:
            third[da] = send(
                outer_out.at[da - 1],
                outer_box.at[da - 1],
                (sem_a.at[0, da], sem_a.at[1, da]),
                device((a + da) % outer, b, c),
            )
    for da in range(1, outer):
        third[da].wait_recv()
        for part in range(2):
            outs[part][...] += outer_box[da - 1, part].astype(jnp.float32)
    for copy in list(first.values()) + list(second.values()) + list(third.values()):
        copy.wait_send()


def spread(own, images, hot, ctf, devices):
    outer, middle = split_axes(devices)
    return pl.pallas_call(
        functools.partial(spread_kernel, devices),
        out_shape=(
            jax.ShapeDtypeStruct((devices,) + own.shape, own.dtype),
            jax.ShapeDtypeStruct(images.shape, images.dtype),
        ),
        in_specs=[pl.BlockSpec(memory_space=VMEM)] * 4,
        out_specs=(pl.BlockSpec(memory_space=VMEM),) * 2,
        scratch_shapes=[
            pltpu.SemaphoreType.DMA((2, outer)),
            pltpu.SemaphoreType.DMA((2, outer, middle)),
            pltpu.SemaphoreType.DMA((2, outer, middle)),
            pltpu.SemaphoreType.DMA,
        ],
        compiler_params=pltpu.CompilerParams(
            collective_id=0, has_side_effects=True, vmem_limit_bytes=24 << 20
        ),
        name="spread",
    )(own, images, hot, ctf)


def collect(keep, leave, devices, capacity):
    outer, middle = split_axes(devices)
    shape = (2, middle, outer, capacity, BW)
    box = (middle, 2, outer, capacity, BW)
    most = max(1, middle - 1)
    return pl.pallas_call(
        functools.partial(collect_kernel, devices),
        out_shape=(jax.ShapeDtypeStruct((capacity, BW), jnp.float32),) * 2,
        in_specs=[pl.BlockSpec(memory_space=pl.ANY)] * 2,
        out_specs=(pl.BlockSpec(memory_space=VMEM),) * 2,
        scratch_shapes=[
            VMEM(box, jnp.float32),
            VMEM(box, jnp.bfloat16),
            VMEM((most, outer, 2, capacity, BW), jnp.bfloat16),
            VMEM((most, outer, 2, capacity, BW), jnp.bfloat16),
            VMEM((max(1, outer - 1), 2, capacity, BW), jnp.bfloat16),
            VMEM((max(1, outer - 1), 2, capacity, BW), jnp.bfloat16),
            pltpu.SemaphoreType.DMA((middle, 2)),
            pltpu.SemaphoreType.DMA((2, middle, 2)),
            pltpu.SemaphoreType.DMA((2, middle, outer)),
            pltpu.SemaphoreType.DMA((2, outer)),
        ],
        compiler_params=pltpu.CompilerParams(
            collective_id=1, has_side_effects=True, vmem_limit_bytes=40 << 20
        ),
        name="collect",
    )(keep.reshape(shape), leave.reshape(shape))


def per_device(images, groups, shifts, volume, owner, local, table_id, interp, ctf):
    devices = lax.axis_size("img")
    block_count = R * KB
    count = images.shape[0]
    blocks = volume.shape[0]
    tries = shifts.shape[0]
    capacity = max(2, 3 * block_count // (2 * devices))
    slots = devices * capacity
    owners = owner[:, 0]

    lines = block_count // BW
    own_slices, target, slot_local, slot_table = pl.pallas_call(
        functools.partial(prep_kernel, devices),
        out_shape=(
            jax.ShapeDtypeStruct((capacity, 2 * BW), jnp.bfloat16),
            jax.ShapeDtypeStruct((lines, BW), jnp.int32),
            jax.ShapeDtypeStruct((1, capacity), jnp.int32),
            jax.ShapeDtypeStruct((capacity, 1), jnp.int32),
        ),
        name="prep",
    )(
        owners.reshape(lines, BW),
        local.reshape(lines, BW),
        table_id.reshape(lines, BW),
        volume,
        interp,
    )
    target = target.reshape(block_count)

    hot = (groups[:, None] == jnp.arange(ctf.shape[0])[None, :]).astype(jnp.float32)
    gathered, weighted = spread(own_slices, images, hot, ctf, devices)
    gathered = gathered.reshape(slots, 2 * BW)
    cosine, sine = phases(shifts)

    keep, leave, evidence = pl.pallas_call(
        main_kernel,
        out_shape=(
            jax.ShapeDtypeStruct((2, slots // 2, BW), jnp.float32),
            jax.ShapeDtypeStruct((2, slots // 2, BW), jnp.bfloat16),
            jax.ShapeDtypeStruct((1, count), jnp.float32),
        ),
        in_specs=[pl.BlockSpec(memory_space=pltpu.SMEM)]
        + [pl.BlockSpec(memory_space=VMEM)] * 6,
        out_specs=(
            pl.BlockSpec(memory_space=pl.ANY),
            pl.BlockSpec(memory_space=VMEM),
            pl.BlockSpec(memory_space=VMEM),
        ),
        scratch_shapes=[
            VMEM((slots, 2 * BW), jnp.float32),
            VMEM((slots, BW), jnp.float32),
            VMEM((slots, BW), jnp.float32),
            VMEM((2 * GROUP, R, BW), jnp.float32),
            VMEM((2 * GROUP, R, BW), jnp.float32),
            VMEM((R, KB * BW), jnp.float32),
            VMEM((tries * R, GROUP * 2 * BW), jnp.bfloat16),
            VMEM((tries * R, GROUP * 2 * BW), jnp.bfloat16),
            VMEM((tries * R, count), jnp.float32),
            VMEM((tries * R, count), jnp.bfloat16),
            pltpu.SemaphoreType.DMA((2,)),
        ],
        compiler_params=pltpu.CompilerParams(vmem_limit_bytes=48 << 20),
        name="score",
    )(target, gathered, weighted, hot, ctf, cosine, sine)

    received_real, received_imag = collect(keep, leave, devices, capacity)
    new_map = pl.pallas_call(
        end_kernel,
        out_shape=jax.ShapeDtypeStruct((blocks, 2 * BW), jnp.float32),
        name="finish",
    )(slot_local, slot_table, received_real, received_imag, volume, interp)
    return (new_map, evidence.reshape(count))


def solution(mesh):
    return jax.shard_map(
        per_device,
        mesh=mesh,
        in_specs=(
            P(("parts", "img"), None),
            P(("parts", "img")),
            P("parts", None),
            P(("parts", "img"), None),
            P("parts", None),
            P("parts"),
            P("parts"),
            P(),
            P("parts", None),
        ),
        out_specs=(P(("parts", "img"), None), P(("parts", "img"))),
        check_vma=False,
    )
```
